128 devices in a mesh: mem: 8 (over y, core), tile: 16 (over z, x).
Axes of the slice: x: 4, y: 4, z: 4, core: 2. Of those that a mesh axis runs over, the one named last changes fastest.
Arguments:
- solution: float32 [40, 4, 128, 1440], P('mem', None, 'tile'), may hold values from -6 to 6
- residual: float32 [40, 4, 128, 1440], P('mem', None, 'tile')
- direction: float32 [40, 4, 128, 1440], P('mem', None, 'tile')
- ensemble: bfloat16 [40, 4, 128, 1440], P('mem', None, 'tile'), may hold values from -6 to 6
- east_rate: float32 [128, 1440], P('tile'), may hold values from 0.06 to 0.12
- north_rate: float32 [128, 1440], P('tile'), may hold values from 0.18 to 0.36
- sea_mask: int32 [128, 1440], P('tile'), may hold values 0 or 1
- pass_counts: int32 [4], replicated, may hold values from 1 to 4, as said below
- obs_owner: int32 [131072, 1], P(('mem', 'tile')), may hold values from 0 to 127; in each aligned block of 1024 rows (0 to 1023, 1024 to 2047, ...) at most 16 rows name the same one
- obs_cell: int32 [131072], P(('mem', 'tile')), may hold values from 0 to 1439
- obs_level: int32 [131072], P(('mem', 'tile')), may hold values from 0 to 1
- obs_variable: int32 [131072], P(('mem', 'tile')), may hold values from 0 to 1
- obs_error: float32 [131072], P(('mem', 'tile')), may hold values from 0.5 to 2
Outputs:
- updated_solution: float32 [40, 4, 128, 1440], P('mem', None, 'tile')
- updated_residual: float32 [40, 4, 128, 1440], P('mem', None, 'tile')
The draws below stay inside these ranges and needn't reach their ends.
Inputs may be any that keep to these rules, and one draw needn't show every extreme that they name: `pass_counts`: each field takes 1 to 4 passes; some field takes 4 and some field takes 1. `obs_owner`: owners are numbered d = (index along mem) * 16 + (index along tile) of the block of rows and longitudes they hold; the observations of one track segment name one owner at most 16 times, a bound that some block reaches. `obs_cell`: row within the band times 180 plus longitude within the block.
All inputs are finite; a program needn't handle non-finite values. No bound on the sum of `sea_mask` on one device may be relied on, other than what follows from the above.
Results may differ from the reference program's by a relative error of at most 0.0011.
Values may be sent and summed in bfloat16 or wider, within the bound.
A program may use at most 128 MiB of HBM per device.

```python
import math
import jax
import jax.numpy as jnp
import numpy as np
from jax import lax

MEMBERS = 40
LEVELS = 2
VARIABLES = 2
FIELDS = 4
ROWS_DEV = 8
LATS = 128
LONS = 1440
LON_BLOCK = 180
OBS_DEV = 1024
OBS = 131072
CAPACITY = 16
PASSES = 4
ITERS = 2
N_MEM = 8
N_TILE = 16


def rough_field(key):
    key_noise, key_rows, key_cols = jax.random.split(key, 3)
    full_shape = (MEMBERS, FIELDS, LATS, LONS)
    random_part = jax.random.normal(key_noise, full_shape, jnp.float32)
    row_level = jax.random.uniform(key_rows, (MEMBERS, FIELDS, LATS, 1), jnp.float32, -1.0, 1.0)
    col_level = jax.random.uniform(key_cols, (1, 1, 1, LONS), jnp.float32, -1.0, 1.0)
    member_pos = jnp.arange(MEMBERS, dtype=jnp.float32)[:, None, None, None]
    lat_pos = jnp.arange(LATS, dtype=jnp.float32)[None, None, :, None]
    position = (member_pos * LATS + lat_pos) / (MEMBERS * LATS)
    growth = 1.0 + 2.0 * position
    return random_part * jnp.sqrt(growth) * jnp.exp(1.15 * (row_level + col_level)) * 0.5


def draw_residual(key, part):
    return rough_field(jax.random.fold_in(key, 11))


def draw_direction(key, part):
    return rough_field(jax.random.fold_in(key, 23))


def draw_pass_counts(key, part):
    key_counts, key_order = jax.random.split(jax.random.fold_in(key, 37))
    counts = jax.random.randint(key_counts, (FIELDS,), 1, PASSES + 1)
    order = jax.random.permutation(key_order, FIELDS)
    counts = counts.at[order[0]].set(PASSES)
    counts = counts.at[order[1]].set(1)
    return counts.astype(jnp.int32)


def plant(result, own_key, low, top_value):
    longest = result.shape.index(max(result.shape))
    spots = []
    for shift in (0, 1):
        where = [jax.random.randint(jax.random.fold_in(own_key, axis), (), 0, length) for axis, length in enumerate(result.shape)]
        where[longest] = (where[longest] + shift) % result.shape[longest]
        spots.append(tuple(where))
    return result.at[spots[0]].set(low).at[spots[1]].set(top_value)


def shard_levels(rng, extent, shards, least, largest):
    loudness = 1.0
    for axis_at, parts in shards:
        draws = jax.random.uniform(jax.random.fold_in(jax.random.fold_in(rng, 6), axis_at), (parts,), jnp.float32, least / len(shards), largest / len(shards))
        loudness = loudness * jnp.repeat(jnp.exp(draws), extent[axis_at] // parts).reshape((-1,) + (1,) * (len(extent) - 1 - axis_at))
    return loudness


def routed_block(rng, own, number, rows, count, top, bound, lean):
    ranking = jax.random.permutation(rng, count)
    packed, common = shares(count, rows * top, bound, lean, True), shares(count, rows * top, bound, lean, False)
    places = jnp.arange(count)

    def named(sizes, rotation):
        used = int((sizes > 0).sum())
        fixed = max(1, used // 4)
        shifted = fixed + (places - fixed + rotation * (used - fixed)) % max(1, count - fixed)
        return jnp.zeros((count,), jnp.int32).at[ranking[jnp.where(places < fixed, places, shifted)]].set(jnp.asarray(sizes, jnp.int32))

    sizes = jnp.where(number % 4 == 0, named(packed, number // 4), named(common, number - number // 4 - 1))
    mixed = jax.random.permutation(jax.random.fold_in(own, 3), count)
    giver, sink = mixed[0:count // 2 * 2:2], mixed[1:count // 2 * 2:2]
    room = jnp.minimum(sizes[giver] - 1, bound - sizes[sink]) // 2
    room = jnp.where((giver == ranking[0]) | (sink == ranking[0]) | (sizes[sink] == 0), 0, jnp.maximum(room, 0))
    shifted = jax.random.randint(jax.random.fold_in(own, 4), (count // 2,), 0, 1 << 20) % (room + 1)
    sizes = sizes.at[giver].add(-shifted).at[sink].add(shifted)
    items = jnp.searchsorted(jnp.cumsum(sizes), jnp.arange(rows * top), side="right").astype(jnp.int32)
    table = items.reshape(top, rows).T
    table = table[jax.random.permutation(jax.random.fold_in(own, 1), rows)]
    rotation = jax.random.randint(jax.random.fold_in(own, 2), (rows, 1), 0, top)
    return jnp.take_along_axis(table, (jnp.arange(top)[None, :] + rotation) % top, axis=1)


def shares(amount, total, bound, lean, full):
    weights = [(1 << 20) // math.isqrt(rank ** lean) + 1 for rank in range(1, amount + 1)]
    largest = bound if full else min(bound, max(-(-total // amount), total * weights[0] // sum(weights)))
    least = 1 if total - largest >= amount - 1 else 0
    given, spare = [largest] + [least] * (amount - 1), total - largest - least * (amount - 1)
    while spare > 0:
        free = [i for i in range(1, amount) if given[i] < largest] or [i for i in range(1, amount) if given[i] < bound]
        pool, remaining = sum([weights[i] for i in free]), spare
        for i in free:
            extra = min(bound - given[i], max(1, remaining * weights[i] // pool), spare)
            given[i] = given[i] + extra
            spare = spare - extra
    return np.array(given)


def bell_draw(key, shape, deviation, limit, pieces=(), kind=jnp.bfloat16):
    entries = jax.random.normal(key, shape, jnp.float32) * deviation
    if len(pieces) > 0:
        entries = shard_levels(key, shape, pieces, -0.22, 0.18) * entries
    return jnp.clip(entries, min=-limit, max=limit).astype(kind)


def setup_inputs(seed: int = 0) -> dict:
    seeds = jax.random.split(jax.random.key(seed), 14)
    solution = bell_draw(seeds[0], (MEMBERS, FIELDS, LATS, LONS), 0.5, 6.0, ((0, 8), (2, 16)), jnp.float32)
    residual = draw_residual(jax.random.fold_in(seeds[13], 71), 0)
    direction = draw_direction(jax.random.fold_in(seeds[13], 71), 0)
    ensemble = bell_draw(seeds[3], (MEMBERS, FIELDS, LATS, LONS), 1.0, 6.0, ((0, 8), (2, 16)))
    east_rate = jnp.clip(jnp.exp(math.log(0.12) - 0.6931472 * jax.random.uniform(seeds[4], (LATS, LONS), jnp.float32) ** shard_levels(seeds[4], (LATS, LONS), ((0, 16),), -0.2, 0.2)), 0.06, 0.12)
    north_rate = jnp.clip(jnp.exp(math.log(0.36) - 0.6931472 * jax.random.uniform(seeds[5], (LATS, LONS), jnp.float32) ** shard_levels(seeds[5], (LATS, LONS), ((0, 16),), -0.2, 0.2)), 0.18, 0.36)
    sea_mask = plant((jax.random.randint(seeds[6], (LATS, LONS), 0, 10) < 7).astype(jnp.int32), jax.random.fold_in(seeds[6], 1), 0, 1)
    pass_counts = draw_pass_counts(jax.random.fold_in(seeds[13], 71), 0)
    obs_owner_keys = jax.random.split(jax.random.fold_in(seeds[8], 1), OBS // OBS_DEV)
    obs_owner_turns = jax.random.permutation(jax.random.fold_in(seeds[8], 3), OBS // OBS_DEV)
    obs_owner = jax.vmap(lambda own, number: routed_block(jax.random.fold_in(seeds[8], 2), own, number, OBS_DEV, N_MEM * N_TILE, 1, CAPACITY, 2))(obs_owner_keys, obs_owner_turns).reshape((OBS, 1))
    obs_cell = plant(jax.random.randint(seeds[9], (OBS,), 0, ROWS_DEV * LON_BLOCK), jax.random.fold_in(seeds[9], 1), 0, (ROWS_DEV * LON_BLOCK) - 1).astype(jnp.int32)
    obs_level = plant(jax.random.randint(seeds[10], (OBS,), 0, LEVELS), jax.random.fold_in(seeds[10], 1), 0, LEVELS - 1).astype(jnp.int32)
    obs_variable = plant(jax.random.randint(seeds[11], (OBS,), 0, VARIABLES), jax.random.fold_in(seeds[11], 1), 0, VARIABLES - 1).astype(jnp.int32)
    obs_error = jnp.clip(jnp.exp(math.log(2.0) - 1.3862944 * jax.random.uniform(seeds[12], (OBS,), jnp.float32) ** shard_levels(seeds[12], (OBS,), ((0, 128),), -0.2, 0.2)), 0.5, 2.0)
    return {"solution": solution, "residual": residual, "direction": direction, "ensemble": ensemble, "east_rate": east_rate, "north_rate": north_rate, "sea_mask": sea_mask, "pass_counts": pass_counts, "obs_owner": obs_owner, "obs_cell": obs_cell, "obs_level": obs_level, "obs_variable": obs_variable, "obs_error": obs_error}


CORRELATION = 0.6

def flow_step(padded, east_faces, north_faces):
    flux_north = north_faces * (padded[..., 1:, :] - padded[..., :-1, :])
    inner = padded[..., 1:-1, :]
    flux_east = east_faces * (jnp.roll(inner, -1, -1) - inner)
    return inner + flux_east - jnp.roll(flux_east, 1, -1) + flux_north[..., 1:, :] - flux_north[..., :-1, :]

def smooth(field, sea, east_faces, north_faces, counts):
    active = field * sea
    for sweep in range(PASSES):
        padded = jnp.pad(active, ((0, 0), (1, 1), (0, 0)))
        moved = flow_step(padded, east_faces, north_faces)
        active = jnp.where(sweep < counts[:, None, None], moved, active)
    return active * sea

def precision_apply(values, errors):
    scaled = values / errors
    length = scaled.shape[-1]
    zero_col = jnp.zeros(scaled.shape[:-1] + (1,), jnp.float32)
    following = jnp.concatenate([scaled[..., 1:], zero_col], -1)
    preceding = jnp.concatenate([zero_col, scaled[..., :-1]], -1)
    position = jnp.arange(length, dtype=jnp.int32)
    at_ends = ((position == 0) | (position == length - 1)).astype(jnp.float32)
    diagonal = 1.0 + CORRELATION * CORRELATION - CORRELATION * CORRELATION * at_ends
    mixed = (diagonal * scaled - CORRELATION * (following + preceding)) / (1.0 - CORRELATION * CORRELATION)
    return mixed / errors

def reference(solution, residual, direction, ensemble, east_rate, north_rate, sea_mask, pass_counts, obs_owner, obs_cell, obs_level, obs_variable, obs_error):
    sea = sea_mask.astype(jnp.float32)
    sea_below = jnp.concatenate([sea[1:], jnp.zeros_like(sea[:1])], 0)
    east_faces = east_rate * sea * jnp.roll(sea, -1, 1)
    north_faces = jnp.concatenate([jnp.zeros_like(sea[:1]), north_rate * sea * sea_below], 0)
    weight = 1.0 / math.sqrt(MEMBERS - 1)
    owners = obs_owner[:, 0]
    lat_index = (owners % N_TILE * ROWS_DEV + obs_cell // LON_BLOCK).astype(jnp.int32)
    lon_index = (owners // N_TILE * LON_BLOCK + obs_cell % LON_BLOCK).astype(jnp.int32)
    field_index = (obs_variable * LEVELS + obs_level).astype(jnp.int32)
    track_errors = obs_error.reshape(N_MEM * N_TILE, OBS_DEV)

    def hessian(vector):

        def forward(carry, pair):
            member_field, member_pert = pair
            shaped = smooth(member_field, sea, east_faces, north_faces, pass_counts).astype(jnp.bfloat16)
            return (carry + member_pert.astype(jnp.float32) * shaped.astype(jnp.float32), None)
        summed, _ = lax.scan(forward, jnp.zeros((FIELDS, LATS, LONS), jnp.float32), (vector, ensemble))
        increment = summed * weight
        obs_value = increment[field_index, lat_index, lon_index]
        weighted = precision_apply(obs_value.reshape(N_MEM * N_TILE, OBS_DEV), track_errors).reshape(-1)
        adjoint = jnp.zeros((FIELDS, LATS, LONS), jnp.float32).at[field_index, lat_index, lon_index].add(weighted)

        def backward(pair):
            member_field, member_pert = pair
            back = (member_pert.astype(jnp.float32) * adjoint * weight).astype(jnp.bfloat16)
            return member_field + smooth(back.astype(jnp.float32), sea, east_faces, north_faces, pass_counts)
        return lax.map(backward, (vector, ensemble))
    norm_now = jnp.sum(residual * residual)
    for iteration in range(ITERS):
        image = hessian(direction)
        step_size = norm_now / jnp.sum(direction * image)
        solution = solution + step_size * direction
        residual = residual - step_size * image
        if iteration + 1 < ITERS:
            norm_next = jnp.sum(residual * residual)
            direction = residual + norm_next / norm_now * direction
            norm_now = norm_next
    return (solution, residual)
```

```python
import functools
import math

import jax
import jax.numpy as jnp
from jax import lax
from jax.experimental import pallas as pl
from jax.experimental.pallas import tpu as pltpu
from jax.sharding import PartitionSpec as P

MESH = pl.DeviceIdType.MESH
F32 = jnp.float32
BF16 = jnp.bfloat16

FIELDS = 4
LEVELS = 2
PASSES = 4
ITERS = 2
CORRELATION = 0.6
MEMBERS_DEV = 5
MEMBERS = 40
ROWS = 8
LONS = 1440
BLOCK = 180
SLOTS = 16
SEGMENT = 1024
NM = 8
NT = 16

HALO = 4
EXT = ROWS + 2 * HALO
PLANES = MEMBERS_DEV * FIELDS
PAD = 24
GROUPS = PAD // 8
WIDE = 1536
OWN = HALO * PAD
EDGE = HALO * PAD
DEVS = NM * NT

IDS = 0


def widen(x):
    return jnp.concatenate([x, x[:, :64], x[:, 1408:1440]], axis=1)


def split(x):
    high = x.astype(BF16).astype(F32)
    return high, x - high


def fold(x, valid):
    total = x[:, 0:128]
    for k in range(1, WIDE // 128 - 1):
        total = total + x[:, 128 * k : 128 * (k + 1)]
    return total + x[:, WIDE - 128 : WIDE] * valid


def row_tile(r, g=0):
    return pl.ds(pl.multiple_of(r * PAD + g * 8, 8), 8)


def body(
    dir_ref,
    res_ref,
    sol_ref,
    ens_ref,
    east_ref,
    north_ref,
    sea_ref,
    counts_ref,
    meta_ref,
    out_sol,
    out_res,
    d_ref,
    r_ref,
    im_ref,
    x_ref,
    y_ref,
    em_ref,
    e_ref,
    n_ref,
    s_ref,
    lb_ref,
    oh_ref,
    rf_ref,
    ct_ref,
    pk_ref,
    ob_ref,
    adj_ref,
    ax_ref,
    one_q,
    one_t,
    pass_ref,
    hs_ref,
    hr_ref,
    as_ref,
    ar_ref,
    cs_ref,
    cr_ref,
    ms_ref,
    mr_ref,
    ts_ref,
    tr_ref,
    h_send,
    h_recv,
    a_send,
    a_recv,
    c_send,
    c_recv,
    m_send,
    m_recv,
    t_send,
    t_recv,
):
    m = lax.axis_index("mem")
    t = lax.axis_index("tile")
    up = lax.rem(t + 1, NT)
    down = lax.rem(t + NT - 1, NT)
    weight = 1.0 / math.sqrt(MEMBERS - 1)

    barrier = pltpu.get_barrier_semaphore()

    def greet_mem(k, _):
        pl.semaphore_signal(
            barrier, inc=1, device_id=(lax.rem(m + k, NM), t), device_id_type=MESH
        )
        return 0

    def greet_tile(k, _):
        pl.semaphore_signal(
            barrier, inc=1, device_id=(m, lax.rem(t + k, NT)), device_id_type=MESH
        )
        return 0

    lax.fori_loop(1, NM, greet_mem, 0)
    lax.fori_loop(1, NT, greet_tile, 0)

    def mem_start(i, pick):
        def one(k, _):
            peer = lax.rem(m + k, NM)
            pltpu.make_async_remote_copy(
                src_ref=ms_ref.at[i, peer if pick else 0],
                dst_ref=mr_ref.at[i, m],
                send_sem=m_send.at[i],
                recv_sem=m_recv.at[i],
                device_id=(peer, t),
                device_id_type=MESH,
            ).start()
            return 0

        lax.fori_loop(1, NM, one, 0)
        mr_ref[i, m] = ms_ref[i, m if pick else 0]

    def mem_wait(i):
        ref = mr_ref.at[i, pl.ds(0, NM - 1)]
        pltpu.make_async_copy(ref, ref, m_recv.at[i]).wait()

    def tile_start(i, pick):
        def one(k, _):
            peer = lax.rem(t + k, NT)
            pltpu.make_async_remote_copy(
                src_ref=ts_ref.at[i, peer if pick else 0],
                dst_ref=tr_ref.at[i, t],
                send_sem=t_send.at[i],
                recv_sem=t_recv.at[i],
                device_id=(m, peer),
                device_id_type=MESH,
            ).start()
            return 0

        lax.fori_loop(1, NT, one, 0)
        tr_ref[i, t] = ts_ref[i, t if pick else 0]

    def tile_wait(i):
        ref = tr_ref.at[i, pl.ds(0, NT - 1)]
        pltpu.make_async_copy(ref, ref, t_recv.at[i]).wait()

    def sides(send, recv, ssem, rsem, i):
        low = pltpu.make_async_remote_copy(
            src_ref=send.at[i, 0],
            dst_ref=recv.at[i, 1],
            send_sem=ssem.at[i, 0],
            recv_sem=rsem.at[i, 1],
            device_id=(m, down),
            device_id_type=MESH,
        )
        high = pltpu.make_async_remote_copy(
            src_ref=send.at[i, 1],
            dst_ref=recv.at[i, 0],
            send_sem=ssem.at[i, 1],
            recv_sem=rsem.at[i, 0],
            device_id=(m, up),
            device_id_type=MESH,
        )
        return low, high

    def sides_start(*which):
        for copy in sides(*which):
            copy.start()

    def sides_wait(*which):
        for copy in sides(*which):
            copy.wait_recv()

    halos = (hs_ref, hr_ref, h_send, h_recv)
    edges = (as_ref, ar_ref, a_send, a_recv)
    faces = (cs_ref, cr_ref, c_send, c_recv)
    DIR, ENS, RES, IMG = 0, 1, 2, 3

    def halo_send(src, kind):
        hs_ref[kind, 0] = src[pl.ds(OWN, EDGE), :].astype(BF16)
        hs_ref[kind, 1] = src[pl.ds(OWN + HALO * PAD, EDGE), :].astype(BF16)
        sides_start(*halos, kind)

    def halo_take(kind, dst):
        dst[pl.ds(0, EDGE), :] = hr_ref[kind, 0].astype(F32)
        dst[pl.ds(OWN + ROWS * PAD, EDGE), :] = hr_ref[kind, 1].astype(F32)

    sub = lax.broadcasted_iota(jnp.int32, (8, WIDE), 0)
    lane = lax.broadcasted_iota(jnp.int32, (8, 128), 1)
    valid = (lane < LONS - (WIDE - 128)).astype(F32)
    sub_small = lax.broadcasted_iota(jnp.int32, (8, 128), 0)
    low_half = sub < 4

    sea = widen(sea_ref[...].astype(F32))
    east = widen(east_ref[...])
    north = widen(north_ref[...])
    sea_up = pltpu.roll(sea, 7, 0)
    east_face = east * sea * pltpu.roll(sea, WIDE - 1, 1)
    north_raw = north * sea
    north_face = jnp.where(sub < 7, north_raw * sea_up, north_raw)
    cs_ref[0, 1] = jnp.where(low_half, pltpu.roll(east_face, 4, 0), north_face)
    cs_ref[0, 0] = jnp.where(
        low_half, east_face, jnp.where(sub < 7, pltpu.roll(north_face, 4, 0), sea_up)
    )

    def spread_row(value, i):
        return jnp.broadcast_to(value[i : i + 1, :], (8, WIDE))

    for i in range(ROWS):
        e_ref[pl.ds((HALO + i) * 8, 8), :] = spread_row(east_face, i)
        n_ref[pl.ds((HALO + i) * 8, 8), :] = spread_row(north_face, i)
        s_ref[pl.ds(i * 8, 8), :] = spread_row(sea, i)

    field_of = lax.rem(sub_small, 4)
    c0, c1, c2, c3 = (counts_ref[0], counts_ref[1], counts_ref[2], counts_ref[3])
    count = jnp.where(
        field_of == 0, c0, jnp.where(field_of == 1, c1, jnp.where(field_of == 2, c2, c3))
    )
    for k in range(PASSES):
        pass_ref[k] = (count > k).astype(F32)

    zero_tile = jnp.zeros((8, WIDE), F32)

    def rows_first(ref, g):
        parts = [widen(ref[8 * g + i].astype(F32)) for i in range(min(8, PLANES - 8 * g))]
        parts += [zero_tile] * (8 - len(parts))
        return jnp.stack(parts, axis=0).transpose(1, 0, 2)

    def planes_first(ref, g):
        rows = jnp.stack([ref[row_tile(HALO + i, g), :] for i in range(ROWS)], axis=0)
        return rows.transpose(1, 0, 2)[:, :, :LONS]

    def sea_rows(r):
        return s_ref[pl.ds(pl.multiple_of(r * 8, 8), 8), :]

    for g in range(GROUPS):
        turned = rows_first(dir_ref, g)
        for i in range(ROWS):
            d_ref[row_tile(HALO + i, g), :] = turned[i]
            x_ref[row_tile(HALO + i, g), :] = turned[i] * sea_rows(i)

    owner = meta_ref[0:1, :].astype(jnp.int32)
    col_id = meta_ref[1:2, :]
    rf_id = meta_ref[2:3, :]
    inv_err = 1.0 / meta_ref[3:4, :]
    owner_tile = lax.rem(owner, NT)
    owner_mem = owner // NT
    dev_iota = lax.broadcasted_iota(jnp.int32, (DEVS, SEGMENT), 0)
    owns = jnp.where(dev_iota == owner, 1.0, 0.0)
    before = jnp.where(
        lax.broadcasted_iota(jnp.int32, (SEGMENT, SEGMENT), 0)
        < lax.broadcasted_iota(jnp.int32, (SEGMENT, SEGMENT), 1),
        1.0,
        0.0,
    ).astype(BF16)
    ranks = jnp.dot(owns.astype(BF16), before, preferred_element_type=F32)
    slot = jnp.sum(ranks * owns, axis=0, keepdims=True).astype(jnp.int32)
    place = owner_mem * SLOTS + slot
    one_q[...] = jnp.where(dev_iota == place, 1.0, 0.0).astype(BF16)
    t_iota = lax.rem(lax.broadcasted_iota(jnp.int32, (2 * NT, SEGMENT), 0), NT)
    t_is_high = lax.broadcasted_iota(jnp.int32, (2 * NT, SEGMENT), 0) < NT
    one_t[...] = jnp.where(t_iota == owner_tile, 1.0, 0.0)

    def to_table(high, low):
        left = one_t[...] * jnp.where(t_is_high, high, low)
        return lax.dot_general(
            left.astype(BF16), one_q[...], (((1,), (1,)), ((), ())), preferred_element_type=F32
        )

    def tile_rows(i, table):
        for k in range(NT):
            ts_ref[i, k] = jnp.broadcast_to(table[k : k + 1, :], (8, 128))

    def tile_table(i):
        return tr_ref[i][:, 0, :]

    table = to_table(col_id, rf_id)
    tile_rows(IDS, table[NT:] * 256.0 + table[:NT])

    pl.semaphore_wait(barrier, NM + NT - 2)

    sides_start(*faces, 0)
    tile_start(IDS, True)
    halo_send(x_ref, DIR)

    for g in range(GROUPS):
        turned = rows_first(ens_ref, g)
        for i in range(ROWS):
            em_ref[row_tile(HALO + i, g), :] = turned[i] * sea_rows(i)
    halo_send(em_ref, ENS)

    tile_wait(IDS)
    ms_ref[IDS, 0] = tile_table(IDS)
    mem_start(IDS, False)

    for g in range(GROUPS):
        turned = rows_first(res_ref, g)
        for i in range(ROWS):
            r_ref[row_tile(HALO + i, g), :] = turned[i]

    mem_wait(IDS)
    ids = mr_ref[IDS].reshape(DEVS, DEVS).T
    rf_all = jnp.floor(ids * (1.0 / 256.0))
    rf_ref[...] = rf_all.astype(jnp.int32)
    ct_ref[...] = (ids - rf_all * 256.0).astype(jnp.int32)

    col_iota = lax.broadcasted_iota(jnp.int32, (256, 128), 0)

    def build(b, _):
        cols = ct_ref[pl.ds(pl.multiple_of(b * SLOTS, SLOTS), SLOTS), :]
        for s in range(SLOTS):
            oh_ref[b, :, s * 128 : (s + 1) * 128] = jnp.where(
                col_iota == cols[s : s + 1, :], 1.0, 0.0
            ).astype(BF16)
        return 0

    lax.fori_loop(0, NM, build, 0)

    sides_wait(*faces, 0)
    below, above = cr_ref[0, 0], cr_ref[0, 1]
    not_first = jnp.where(t > 0, 1.0, 0.0)
    not_last = jnp.where(t < NT - 1, 1.0, 0.0)
    for i in range(HALO):
        e_ref[pl.ds(i * 8, 8), :] = spread_row(below, i)
        e_ref[pl.ds((HALO + ROWS + i) * 8, 8), :] = spread_row(above, i)
    for i in range(HALO - 1):
        n_ref[pl.ds(i * 8, 8), :] = spread_row(below, HALO + i)
        n_ref[pl.ds((HALO + ROWS + i) * 8, 8), :] = spread_row(above, HALO + i)
    n_ref[pl.ds((HALO - 1) * 8, 8), :] = (
        spread_row(below, 2 * HALO - 1) * s_ref[pl.ds(0, 8), :] * not_first
    )
    n_ref[pl.ds((HALO + ROWS - 1) * 8, 8), :] = (
        n_ref[pl.ds((HALO + ROWS - 1) * 8, 8), :] * spread_row(above, 2 * HALO - 1) * not_last
    )

    def localize():
        for k in range(PASSES):
            src, dst = (x_ref, y_ref) if k % 2 == 0 else (y_ref, x_ref)

            def row(r, _):
                keep = pass_ref[k][:, 0:1]
                here8 = pl.ds(pl.multiple_of(r * 8, 8), 8)
                back8 = pl.ds(pl.multiple_of((r - 1) * 8, 8), 8)
                e, n, s = e_ref[here8, :], n_ref[here8, :], n_ref[back8, :]
                for g in range(GROUPS):
                    a = src[row_tile(r, g), :]
                    flux = e * (pltpu.roll(a, WIDE - 1, 1) - a)
                    moved = (
                        flux
                        - pltpu.roll(flux, 1, 1)
                        + n * (src[row_tile(r + 1, g), :] - a)
                        - s * (a - src[row_tile(r - 1, g), :])
                    )
                    dst[row_tile(r, g), :] = a + keep * moved
                return 0

            lax.fori_loop(1 + k, EXT - 1 - k, row, 0)

    row_key = lax.broadcasted_iota(jnp.int32, (64, 128), 0)
    key = (row_key // 8) * FIELDS + lax.rem(row_key, 4)
    is_high = lax.rem(row_key, 8) < 4

    def window(b):
        start = BLOCK * b
        first = (start // 128) * 128
        return first, start - first

    dots = []
    norms = None
    for iteration in range(ITERS):
        base = 1 + 3 * iteration
        PICK, WGT, SUM = base, base + 1, base + 2
        if iteration == 0:
            sides_wait(*halos, DIR)
            halo_take(DIR, x_ref)
        localize()

        def partial(r, _):
            total = zero_tile
            for g in range(GROUPS):
                at = row_tile(r + HALO, g)
                total = total + em_ref[at, :] * x_ref[at, :].astype(BF16).astype(F32)
            total = total + pltpu.roll(total, 4, 0)
            high, low = split(total)
            adj_ref[pl.ds(pl.multiple_of(r * 8, 8), 8), :] = jnp.where(low_half, high, low)
            return 0

        lax.fori_loop(0, ROWS, partial, 0)
        for b in range(NM):
            first, shift = window(b)
            piece = adj_ref[:, first : first + 384]
            if shift:
                piece = pltpu.roll(piece, 384 - shift, 1)
            lb_ref[b] = piece[:, :256].astype(BF16)

        def gather(b, _):
            got = jnp.dot(lb_ref[b], oh_ref[b], preferred_element_type=F32)
            rows16 = pl.ds(pl.multiple_of(b * SLOTS, SLOTS), SLOTS)
            wanted = rf_ref[rows16, :]
            rows = []
            for s in range(SLOTS):
                part = jnp.where(
                    key == wanted[s : s + 1, :], got[:, s * 128 : (s + 1) * 128], 0.0
                )
                rows.append(jnp.sum(part, axis=0, keepdims=True))
            pk_ref[rows16, :] = jnp.concatenate(rows, axis=0)
            return 0

        lax.fori_loop(0, NM, gather, 0)
        ms_ref[PICK] = pk_ref[...].T.reshape(NM, NT, 128)
        mem_start(PICK, True)
        mem_wait(PICK)
        summed = mr_ref[PICK, 0]
        for k in range(1, NM):
            summed = summed + mr_ref[PICK, k]
        tile_rows(PICK, summed * weight)
        tile_start(PICK, True)
        if iteration == 0:
            def mask_residual(r, _):
                sea_row = s_ref[pl.ds(pl.multiple_of(r * 8, 8), 8), :]
                for g in range(GROUPS):
                    at = row_tile(r + HALO, g)
                    y_ref[at, :] = r_ref[at, :] * sea_row
                return 0

            lax.fori_loop(0, ROWS, mask_residual, 0)
        tile_wait(PICK)

        high, low = split(tile_table(PICK))
        both = jnp.concatenate([high, low], axis=0).astype(BF16)
        seen = jnp.dot(both, one_q[...], preferred_element_type=F32)
        value = jnp.sum(seen * one_t[...], axis=0, keepdims=True)
        u = value * inv_err
        along = lax.broadcasted_iota(jnp.int32, (1, SEGMENT), 1)
        following = jnp.where(along == SEGMENT - 1, 0.0, pltpu.roll(u, SEGMENT - 1, 1))
        preceding = jnp.where(along == 0, 0.0, pltpu.roll(u, 1, 1))
        ends = ((along == 0) | (along == SEGMENT - 1)).astype(F32)
        square = CORRELATION * CORRELATION
        mixed = ((1.0 + square - square * ends) * u - CORRELATION * (following + preceding)) / (
            1.0 - square
        )
        weighted = mixed * inv_err
        high, low = split(weighted)
        table = to_table(high, low)
        tile_rows(WGT, table[:NT] + table[NT:])
        tile_start(WGT, True)
        if iteration == 0:
            halo_send(y_ref, RES)
        tile_wait(WGT)
        ms_ref[WGT, 0] = tile_table(WGT)
        mem_start(WGT, False)
        mem_wait(WGT)
        pk_ref[...] = mr_ref[WGT].reshape(DEVS, DEVS).T

        def scatter(b, _):
            rows16 = pl.ds(pl.multiple_of(b * SLOTS, SLOTS), SLOTS)
            wanted = rf_ref[rows16, :]
            high, low = split(pk_ref[rows16, :])
            parts = []
            for s in range(SLOTS):
                row = jnp.where(is_high, high[s : s + 1, :], low[s : s + 1, :])
                parts.append(jnp.where(key == wanted[s : s + 1, :], row, 0.0).astype(BF16))
            ob_ref[b] = lax.dot_general(
                jnp.concatenate(parts, axis=1),
                oh_ref[b],
                (((1,), (1,)), ((), ())),
                preferred_element_type=F32,
            )
            return 0

        lax.fori_loop(0, NM, scatter, 0)
        adj_ref[...] = jnp.zeros((64, WIDE), F32)
        for b in range(NM):
            first, shift = window(b)
            piece = jnp.concatenate([ob_ref[b], jnp.zeros((64, 128), F32)], axis=1)
            if shift:
                piece = pltpu.roll(piece, shift, 1)
            adj_ref[:, first : first + 384] = adj_ref[:, first : first + 384] + piece
        lane64 = lax.broadcasted_iota(jnp.int32, (64, 128), 1)
        head, tail = adj_ref[:, 0:128], adj_ref[:, WIDE - 128 : WIDE]
        adj_ref[:, WIDE - 128 : WIDE] = jnp.where(
            lane64 < 32, tail, jnp.where(lane64 < 96, pltpu.roll(head, 32, 1), pltpu.roll(tail, 96, 1))
        )
        own_rows = []
        for i in range(ROWS):
            tile = adj_ref[pl.ds(i * 8, 8), :]
            tile = (tile + pltpu.roll(tile, 4, 0)) * weight
            ax_ref[pl.ds((HALO + i) * 8, 8), :] = tile
        for side in range(2):
            for i in range(HALO // 2):
                first = HALO + HALO * side + 2 * i
                as_ref[iteration, side, pl.ds(i * 8, 8), :] = jnp.where(
                    low_half,
                    ax_ref[pl.ds(first * 8, 8), :],
                    ax_ref[pl.ds((first + 1) * 8, 8), :],
                )
        sides_start(*edges, iteration)
        if iteration == 0:
            sides_wait(*halos, ENS)
            halo_take(ENS, em_ref)
        sides_wait(*edges, iteration)
        for side in range(2):
            for i in range(HALO // 2):
                first = (HALO + ROWS) * side + 2 * i
                packed = ar_ref[iteration, side, pl.ds(i * 8, 8), :]
                turned = pltpu.roll(packed, 4, 0)
                ax_ref[pl.ds(first * 8, 8), :] = jnp.where(low_half, packed, turned)
                ax_ref[pl.ds((first + 1) * 8, 8), :] = jnp.where(low_half, turned, packed)

        def back(r, _):
            row = ax_ref[pl.ds(pl.multiple_of(r * 8, 8), 8), :]
            for g in range(GROUPS):
                at = row_tile(r, g)
                x_ref[at, :] = (em_ref[at, :] * row).astype(BF16).astype(F32)
            return 0

        lax.fori_loop(0, EXT, back, 0)
        localize()

        def image(r, carry):
            sea_row = s_ref[pl.ds(pl.multiple_of(r * 8, 8), 8), :]
            sums = list(carry)
            for g in range(GROUPS):
                at = row_tile(r + HALO, g)
                d, res = d_ref[at, :], r_ref[at, :]
                moved = sea_row * x_ref[at, :]
                img = d + moved
                im_ref[at, :] = img
                if iteration == 0:
                    y_ref[at, :] = img * sea_row
                terms = [d * img, res * res]
                if iteration == 0:
                    terms += [res * img, img * img]
                sums = [total + fold(term, valid) for total, term in zip(sums, terms)]
            return tuple(sums)

        count_sums = 4 if iteration == 0 else 2
        sums = lax.fori_loop(0, ROWS, image, (jnp.zeros((8, 128), F32),) * count_sums)
        packed = jnp.zeros((8, 128), F32)
        for i, total in enumerate(sums):
            packed = jnp.where(sub_small == i, jnp.sum(total, axis=0, keepdims=True), packed)
        ms_ref[SUM, 0, pl.ds(0, 8), :] = packed
        ms_ref[SUM, 0, pl.ds(8, 8), :] = packed
        mem_start(SUM, False)
        if iteration == 0:
            halo_send(y_ref, IMG)
        mem_wait(SUM)
        part = mr_ref[SUM, 0, pl.ds(0, 8), :]
        for k in range(1, NM):
            part = part + mr_ref[SUM, k, pl.ds(0, 8), :]
        ts_ref[SUM, 0] = part
        tile_start(SUM, False)
        tile_wait(SUM)
        total = tr_ref[SUM, 0]
        for k in range(1, NT):
            total = total + tr_ref[SUM, k]
        total = jnp.sum(total, axis=1, keepdims=True)
        d_image, rr = total[0:1, :], total[1:2, :]
        step = rr / d_image
        if iteration == 0:
            r_image, image_image = total[2:3, :], total[3:4, :]
            fresh = rr - 2.0 * step * r_image + step * step * image_image
            beta = fresh / rr
            first_step = step
            for p in range(PLANES):
                out_sol[p] = sol_ref[p] + step * dir_ref[p]
            sides_wait(*halos, RES)
            sides_wait(*halos, IMG)
            for side in range(2):
                for i in range(HALO):
                    inner = pl.ds(i * PAD, PAD)
                    outer = pl.ds(side * (OWN + ROWS * PAD) + i * PAD, PAD)
                    mixed = (
                        hr_ref[RES, side, inner, :].astype(F32)
                        - step * hr_ref[IMG, side, inner, :].astype(F32)
                        + beta * hr_ref[DIR, side, inner, :].astype(F32)
                    )
                    x_ref[outer, :] = mixed

            def turn(r, _):
                sea_row = s_ref[pl.ds(pl.multiple_of(r * 8, 8), 8), :]
                for g in range(GROUPS):
                    at = row_tile(r + HALO, g)
                    res = r_ref[at, :] - step * im_ref[at, :]
                    r_ref[at, :] = res
                    fresh_dir = res + beta * d_ref[at, :]
                    d_ref[at, :] = fresh_dir
                    x_ref[at, :] = fresh_dir * sea_row
                return 0

            lax.fori_loop(0, ROWS, turn, 0)
        else:

            for g in range(GROUPS):
                d = planes_first(d_ref, g)
                res = planes_first(r_ref, g)
                img = planes_first(im_ref, g)
                for i in range(min(8, PLANES - 8 * g)):
                    p = 8 * g + i
                    out_sol[p] = out_sol[p] + step * d[i]
                    out_res[p] = res[i] - step * img[i]

    for i in range(1 + 3 * ITERS):
        ref = mr_ref.at[i, pl.ds(0, NM - 1)]
        pltpu.make_async_copy(ref, ref, m_send.at[i]).wait()
        ref = tr_ref.at[i, pl.ds(0, NT - 1)]
        pltpu.make_async_copy(ref, ref, t_send.at[i]).wait()
    for group, many in ((halos, 4), (edges, ITERS), (faces, 1)):
        for i in range(many):
            for copy in sides(*group, i):
                copy.wait_send()


def shards(
    solution,
    residual,
    direction,
    ensemble,
    east_rate,
    north_rate,
    sea_mask,
    pass_counts,
    obs_owner,
    obs_cell,
    obs_level,
    obs_variable,
    obs_error,
):
    def planes(x):
        return x.reshape(PLANES, ROWS, LONS)

    row, col = obs_cell // BLOCK, obs_cell % BLOCK
    key = row * FIELDS + obs_variable * LEVELS + obs_level
    meta = jnp.stack(
        [obs_owner[:, 0].astype(F32), col.astype(F32), key.astype(F32), obs_error], axis=0
    )
    exchanges = 1 + 3 * ITERS
    vmem = pl.BlockSpec(memory_space=pltpu.VMEM)
    field = pltpu.VMEM((EXT * PAD, WIDE), F32)
    band = pltpu.VMEM((EXT * 8, WIDE), F32)
    shape = jax.ShapeDtypeStruct((PLANES, ROWS, LONS), F32)
    sol, res = pl.pallas_call(
        body,
        out_shape=(shape, shape),
        in_specs=[vmem] * 7 + [pl.BlockSpec(memory_space=pltpu.SMEM), vmem],
        out_specs=(vmem, vmem),
        scratch_shapes=[
            field,
            field,
            field,
            field,
            field,
            field,
            band,
            band,
            pltpu.VMEM((ROWS * 8, WIDE), F32),
            pltpu.VMEM((NM, 64, 256), BF16),
            pltpu.VMEM((NM, 256, SLOTS * 128), BF16),
            pltpu.VMEM((DEVS, 128), jnp.int32),
            pltpu.VMEM((DEVS, 128), jnp.int32),
            pltpu.VMEM((DEVS, 128), F32),
            pltpu.VMEM((NM, 64, 256), F32),
            pltpu.VMEM((64, WIDE), F32),
            band,
            pltpu.VMEM((DEVS, SEGMENT), BF16),
            pltpu.VMEM((2 * NT, SEGMENT), F32),
            pltpu.VMEM((PASSES, 8, 128), F32),
            pltpu.VMEM((4, 2, EDGE, WIDE), BF16),
            pltpu.VMEM((4, 2, EDGE, WIDE), BF16),
            pltpu.VMEM((ITERS, 2, 16, WIDE), F32),
            pltpu.VMEM((ITERS, 2, 16, WIDE), F32),
            pltpu.VMEM((1, 2, 8, WIDE), F32),
            pltpu.VMEM((1, 2, 8, WIDE), F32),
            pltpu.VMEM((exchanges, NM, NT, 128), F32),
            pltpu.VMEM((exchanges, NM, NT, 128), F32),
            pltpu.VMEM((exchanges, NT, 8, 128), F32),
            pltpu.VMEM((exchanges, NT, 8, 128), F32),
            pltpu.SemaphoreType.DMA((4, 2)),
            pltpu.SemaphoreType.DMA((4, 2)),
            pltpu.SemaphoreType.DMA((ITERS, 2)),
            pltpu.SemaphoreType.DMA((ITERS, 2)),
            pltpu.SemaphoreType.DMA((1, 2)),
            pltpu.SemaphoreType.DMA((1, 2)),
            pltpu.SemaphoreType.DMA((exchanges,)),
            pltpu.SemaphoreType.DMA((exchanges,)),
            pltpu.SemaphoreType.DMA((exchanges,)),
            pltpu.SemaphoreType.DMA((exchanges,)),
        ],
        compiler_params=pltpu.CompilerParams(
            collective_id=0, has_side_effects=True, vmem_limit_bytes=60 * 1024 * 1024
        ),
    )(
        planes(direction),
        planes(residual),
        planes(solution),
        planes(ensemble),
        east_rate,
        north_rate,
        sea_mask,
        pass_counts,
        meta,
    )
    return sol.reshape(solution.shape), res.reshape(solution.shape)


def solution(mesh):
    return jax.shard_map(
        shards,
        mesh=mesh,
        in_specs=(
            P("mem", None, "tile", None),
            P("mem", None, "tile", None),
            P("mem", None, "tile", None),
            P("mem", None, "tile", None),
            P("tile", None),
            P("tile", None),
            P("tile", None),
            P(),
            P(("mem", "tile"), None),
            P(("mem", "tile")),
            P(("mem", "tile")),
            P(("mem", "tile")),
            P(("mem", "tile")),
        ),
        out_specs=(P("mem", None, "tile", None), P("mem", None, "tile", None)),
        check_vma=False,
    )
```

```python
import functools
import math

import jax
import jax.numpy as jnp
from jax import lax
from jax.experimental import pallas as pl
from jax.experimental.pallas import tpu as pltpu
from jax.sharding import PartitionSpec as P

MESH = pl.DeviceIdType.MESH
F32 = jnp.float32
BF16 = jnp.bfloat16

FIELDS = 4
LEVELS = 2
PASSES = 4
ITERS = 2
CORRELATION = 0.6
MEMBERS_DEV = 5
MEMBERS = 40
ROWS = 8
LONS = 1440
BLOCK = 180
SLOTS = 16
SEGMENT = 1024
NM = 8
NT = 16

HALO = 4
EXT = ROWS + 2 * HALO
PLANES = MEMBERS_DEV * FIELDS
PAD = 24
GROUPS = PAD // 8
WIDE = 1536
OWN = HALO * PAD
EDGE = HALO * PAD
DEVS = NM * NT
LIMIT = 60 * 1024 * 1024
TILES = WIDE // 128

IDS = 0


def widen(x):
    return jnp.concatenate([x, x[:, :64], x[:, 1408:1440]], axis=1)


def split(x):
    high = x.astype(BF16).astype(F32)
    return high, x - high


def fold(x, valid):
    total = x[:, 0:128]
    for k in range(1, WIDE // 128 - 1):
        total = total + x[:, 128 * k : 128 * (k + 1)]
    return total + x[:, WIDE - 128 : WIDE] * valid


def cols_of(j):
    return slice(128 * j, 128 * (j + 1))


def row_tile(r, g=0):
    return pl.ds(pl.multiple_of(r * PAD + g * 8, 8), 8)


def body(
    dir_hbm,
    res_hbm,
    sol_hbm,
    ens_hbm,
    east_hbm,
    north_hbm,
    sea_hbm,
    counts_ref,
    owner_hbm,
    cell_hbm,
    level_hbm,
    variable_hbm,
    error_hbm,
    out_sol,
    out_res,
    dir_ref,
    res_ref,
    sol_ref,
    ens_ref,
    east_ref,
    north_ref,
    sea_ref,
    owner_ref,
    cell_ref,
    level_ref,
    variable_ref,
    error_ref,
    load_sem,
    d_ref,
    r_ref,
    im_ref,
    x_ref,
    p1_ref,
    p2_ref,
    p3_ref,
    z_ref,
    l0_ref,
    lr_ref,
    em_ref,
    e_ref,
    n_ref,
    w_ref,
    k_ref,
    s_ref,
    lb_ref,
    oh_ref,
    rf_ref,
    ct_ref,
    pk_ref,
    ob_ref,
    adj_ref,
    ax_ref,
    one_q,
    one_t,
    pass_ref,
    hs_ref,
    hr_ref,
    as_ref,
    ar_ref,
    cs_ref,
    cr_ref,
    ms_ref,
    mr_ref,
    ts_ref,
    tr_ref,
    h_send,
    h_recv,
    a_send,
    a_recv,
    c_send,
    c_recv,
    m_send,
    m_recv,
    t_send,
    t_recv,
):
    m = lax.axis_index("mem")
    t = lax.axis_index("tile")
    up = lax.rem(t + 1, NT)
    down = lax.rem(t + NT - 1, NT)
    weight = 1.0 / math.sqrt(MEMBERS - 1)

    loads = {}
    for i, (name, source, target) in enumerate(
        (
            ("dir", dir_hbm, dir_ref),
            ("sea", sea_hbm, sea_ref),
            ("east", east_hbm, east_ref),
            ("north", north_hbm, north_ref),
            ("owner", owner_hbm, owner_ref),
            ("cell", cell_hbm, cell_ref),
            ("level", level_hbm, level_ref),
            ("variable", variable_hbm, variable_ref),
            ("error", error_hbm, error_ref),
            ("ens", ens_hbm, ens_ref),
            ("res", res_hbm, res_ref),
            ("sol", sol_hbm, sol_ref),
        )
    ):
        loads[name] = pltpu.make_async_copy(source, target, load_sem.at[i])
        loads[name].start()

    def loaded(*which):
        for name in which:
            loads[name].wait()

    barrier = pltpu.get_barrier_semaphore()

    def greet_mem(k, _):
        pl.semaphore_signal(
            barrier, inc=1, device_id=(lax.rem(m + k, NM), t), device_id_type=MESH
        )
        return 0

    def greet_tile(k, _):
        pl.semaphore_signal(
            barrier, inc=1, device_id=(m, lax.rem(t + k, NT)), device_id_type=MESH
        )
        return 0

    lax.fori_loop(1, NM, greet_mem, 0)
    lax.fori_loop(1, NT, greet_tile, 0)

    def mem_start(i, pick):
        def one(k, _):
            peer = lax.rem(m + k, NM)
            pltpu.make_async_remote_copy(
                src_ref=ms_ref.at[i, peer if pick else 0],
                dst_ref=mr_ref.at[i, m],
                send_sem=m_send.at[i],
                recv_sem=m_recv.at[i],
                device_id=(peer, t),
                device_id_type=MESH,
            ).start()
            return 0

        lax.fori_loop(1, NM, one, 0)
        mr_ref[i, m] = ms_ref[i, m if pick else 0]

    def mem_wait(i):
        ref = mr_ref.at[i, pl.ds(0, NM - 1)]
        pltpu.make_async_copy(ref, ref, m_recv.at[i]).wait()

    def tile_start(i, pick):
        def one(k, _):
            peer = lax.rem(t + k, NT)
            pltpu.make_async_remote_copy(
                src_ref=ts_ref.at[i, peer if pick else 0],
                dst_ref=tr_ref.at[i, t],
                send_sem=t_send.at[i],
                recv_sem=t_recv.at[i],
                device_id=(m, peer),
                device_id_type=MESH,
            ).start()
            return 0

        lax.fori_loop(1, NT, one, 0)
        tr_ref[i, t] = ts_ref[i, t if pick else 0]

    def tile_wait(i):
        ref = tr_ref.at[i, pl.ds(0, NT - 1)]
        pltpu.make_async_copy(ref, ref, t_recv.at[i]).wait()

    def sides(send, recv, ssem, rsem, i):
        low = pltpu.make_async_remote_copy(
            src_ref=send.at[i, 0],
            dst_ref=recv.at[i, 1],
            send_sem=ssem.at[i, 0],
            recv_sem=rsem.at[i, 1],
            device_id=(m, down),
            device_id_type=MESH,
        )
        high = pltpu.make_async_remote_copy(
            src_ref=send.at[i, 1],
            dst_ref=recv.at[i, 0],
            send_sem=ssem.at[i, 1],
            recv_sem=rsem.at[i, 0],
            device_id=(m, up),
            device_id_type=MESH,
        )
        return low, high

    def sides_start(*which):
        for copy in sides(*which):
            copy.start()

    def sides_wait(*which):
        for copy in sides(*which):
            copy.wait_recv()

    edges = (as_ref, ar_ref, a_send, a_recv)
    faces = (cs_ref, cr_ref, c_send, c_recv)
    DIR, ENS, RES, IMG = 0, 1, 2, 3

    def halo_piece(kind, dist):
        low = pltpu.make_async_remote_copy(
            src_ref=hs_ref.at[kind, 0, dist - 1],
            dst_ref=hr_ref.at[kind, 1, dist - 1],
            send_sem=h_send.at[kind, dist - 1, 0],
            recv_sem=h_recv.at[kind, dist - 1, 1],
            device_id=(m, down),
            device_id_type=MESH,
        )
        high = pltpu.make_async_remote_copy(
            src_ref=hs_ref.at[kind, 1, dist - 1],
            dst_ref=hr_ref.at[kind, 0, dist - 1],
            send_sem=h_send.at[kind, dist - 1, 1],
            recv_sem=h_recv.at[kind, dist - 1, 0],
            device_id=(m, up),
            device_id_type=MESH,
        )
        return low, high

    def below_row(dist):
        return HALO - dist

    def above_row(dist):
        return HALO + ROWS - 1 + dist

    def whole_row(r):
        return pl.ds(r * PAD, PAD)

    def halo_send(kind, dist, row_of):
        hs_ref[kind, 0, dist - 1] = row_of(HALO + dist - 1).astype(BF16)
        hs_ref[kind, 1, dist - 1] = row_of(HALO + ROWS - dist).astype(BF16)
        for copy in halo_piece(kind, dist):
            copy.start()

    def halo_take(kind, dist, dst):
        for copy in halo_piece(kind, dist):
            copy.wait_recv()
        dst[whole_row(below_row(dist)), :] = hr_ref[kind, 0, dist - 1].astype(F32)
        dst[whole_row(above_row(dist)), :] = hr_ref[kind, 1, dist - 1].astype(F32)

    sub = lax.broadcasted_iota(jnp.int32, (8, WIDE), 0)
    lane = lax.broadcasted_iota(jnp.int32, (8, 128), 1)
    valid = (lane < LONS - (WIDE - 128)).astype(F32)
    sub_small = lax.broadcasted_iota(jnp.int32, (8, 128), 0)
    low_half = sub < 4
    is_first, is_last = lane == 0, lane == 127

    loaded("sea", "east", "north")
    sea = widen(sea_ref[...].astype(F32))
    east = widen(east_ref[...])
    north = widen(north_ref[...])
    sea_up = pltpu.roll(sea, 7, 0)
    east_face = east * sea * pltpu.roll(sea, WIDE - 1, 1)
    north_raw = north * sea
    north_face = jnp.where(sub < 7, north_raw * sea_up, north_raw)
    cs_ref[0, 1] = jnp.where(low_half, pltpu.roll(east_face, 4, 0), north_face)
    cs_ref[0, 0] = jnp.where(
        low_half, east_face, jnp.where(sub < 7, pltpu.roll(north_face, 4, 0), sea_up)
    )

    def spread_row(value, i):
        return jnp.broadcast_to(value[i : i + 1, :], (8, WIDE))

    for i in range(ROWS):
        e_ref[pl.ds((HALO + i) * 8, 8), :] = spread_row(east_face, i)
        n_ref[pl.ds((HALO + i) * 8, 8), :] = spread_row(north_face, i)
        s_ref[pl.ds(i * 8, 8), :] = spread_row(sea, i)

    field_of = lax.rem(sub_small, 4)
    c0, c1, c2, c3 = (counts_ref[0], counts_ref[1], counts_ref[2], counts_ref[3])
    count = jnp.where(
        field_of == 0, c0, jnp.where(field_of == 1, c1, jnp.where(field_of == 2, c2, c3))
    )
    for k in range(PASSES):
        pass_ref[k] = (count > k).astype(F32)

    zero_tile = jnp.zeros((8, WIDE), F32)

    def rows_first(ref, g):
        parts = [widen(ref[8 * g + i].astype(F32)) for i in range(min(8, PLANES - 8 * g))]
        parts += [zero_tile] * (8 - len(parts))
        return jnp.stack(parts, axis=0).transpose(1, 0, 2)

    def planes_first(ref, g):
        rows = jnp.stack([ref[row_tile(HALO + i, g), :] for i in range(ROWS)], axis=0)
        return rows.transpose(1, 0, 2)[:, :, :LONS]

    def sea_rows(r):
        return s_ref[pl.ds(pl.multiple_of(r * 8, 8), 8), :]

    loaded("dir")
    for g in range(GROUPS):
        turned = rows_first(dir_ref, g)
        for i in range(ROWS):
            d_ref[row_tile(HALO + i, g), :] = turned[i]
            x_ref[row_tile(HALO + i, g), :] = turned[i] * sea_rows(i)

    pl.semaphore_wait(barrier, NM + NT - 2)

    sides_start(*faces, 0)

    def masked(ref):
        return lambda r: ref[whole_row(r), :]

    halo_send(DIR, 1, masked(x_ref))
    halo_send(DIR, 2, masked(x_ref))

    loaded("owner", "cell", "level", "variable", "error")
    owner = owner_ref[...]
    cell = cell_ref[...].astype(F32)
    cell_row = jnp.floor((cell + 0.5) * (1.0 / BLOCK))
    col_id = cell - cell_row * BLOCK
    rf_id = cell_row * FIELDS + (variable_ref[...] * LEVELS + level_ref[...]).astype(F32)
    inv_err = 1.0 / error_ref[...]
    owner_tile = lax.rem(owner, NT)
    owner_mem = owner // NT
    dev_iota = lax.broadcasted_iota(jnp.int32, (DEVS, SEGMENT), 0)
    owns = jnp.where(dev_iota == owner, 1.0, 0.0)
    before = jnp.where(
        lax.broadcasted_iota(jnp.int32, (SEGMENT, SEGMENT), 0)
        < lax.broadcasted_iota(jnp.int32, (SEGMENT, SEGMENT), 1),
        1.0,
        0.0,
    ).astype(BF16)
    ranks = jnp.dot(owns.astype(BF16), before, preferred_element_type=F32)
    slot = jnp.sum(ranks * owns, axis=0, keepdims=True).astype(jnp.int32)
    place = owner_mem * SLOTS + slot
    one_q[...] = jnp.where(dev_iota == place, 1.0, 0.0).astype(BF16)
    t_iota = lax.rem(lax.broadcasted_iota(jnp.int32, (2 * NT, SEGMENT), 0), NT)
    t_is_high = lax.broadcasted_iota(jnp.int32, (2 * NT, SEGMENT), 0) < NT
    one_t[...] = jnp.where(t_iota == owner_tile, 1.0, 0.0)

    def to_table(high, low):
        left = one_t[...] * jnp.where(t_is_high, high, low)
        return lax.dot_general(
            left.astype(BF16), one_q[...], (((1,), (1,)), ((), ())), preferred_element_type=F32
        )

    def tile_rows(i, table):
        for k in range(NT):
            ts_ref[i, k] = jnp.broadcast_to(table[k : k + 1, :], (8, 128))

    def tile_table(i):
        return tr_ref[i][:, 0, :]

    table = to_table(col_id, rf_id)
    tile_rows(IDS, table[NT:] * 256.0 + table[:NT])

    tile_start(IDS, True)
    halo_send(DIR, 3, masked(x_ref))
    halo_send(DIR, 4, masked(x_ref))

    loaded("res")
    for g in range(GROUPS):
        turned = rows_first(res_ref, g)
        for i in range(ROWS):
            r_ref[row_tile(HALO + i, g), :] = turned[i]
            lr_ref[row_tile(HALO + i, g), :] = turned[i] * sea_rows(i)
    for dist in range(1, HALO + 1):
        halo_send(RES, dist, masked(lr_ref))

    loaded("ens")
    for g in range(GROUPS):
        turned = rows_first(ens_ref, g)
        for i in range(ROWS):
            em_ref[row_tile(HALO + i, g), :] = turned[i] * sea_rows(i)
    for dist in range(1, HALO + 1):
        halo_send(ENS, dist, masked(em_ref))

    sides_wait(*faces, 0)
    below, above = cr_ref[0, 0], cr_ref[0, 1]
    not_first = jnp.where(t > 0, 1.0, 0.0)
    not_last = jnp.where(t < NT - 1, 1.0, 0.0)
    for i in range(HALO):
        e_ref[pl.ds(i * 8, 8), :] = spread_row(below, i)
        e_ref[pl.ds((HALO + ROWS + i) * 8, 8), :] = spread_row(above, i)
    for i in range(HALO - 1):
        n_ref[pl.ds(i * 8, 8), :] = spread_row(below, HALO + i)
        n_ref[pl.ds((HALO + ROWS + i) * 8, 8), :] = spread_row(above, HALO + i)
    n_ref[pl.ds((HALO - 1) * 8, 8), :] = (
        spread_row(below, 2 * HALO - 1) * s_ref[pl.ds(0, 8), :] * not_first
    )
    n_ref[pl.ds((HALO + ROWS - 1) * 8, 8), :] = (
        n_ref[pl.ds((HALO + ROWS - 1) * 8, 8), :] * spread_row(above, 2 * HALO - 1) * not_last
    )

    for r in range(1, EXT - 1):
        here = pl.ds(r * 8, 8)
        e, n, s = e_ref[here, :], n_ref[here, :], n_ref[pl.ds((r - 1) * 8, 8), :]
        w = pltpu.roll(e, 1, 1)
        w_ref[here, :] = w
        k_ref[here, :] = 1.0 - e - w - n - s

    levels = (x_ref, p1_ref, p2_ref, p3_ref)

    def localization(result):
        def passing(k, first, second):
            src = levels[k]
            dst = levels[k + 1] if k + 1 < PASSES else result
            keep = jnp.broadcast_to(pass_ref[k][:, 0:1], (8, 128)) > 0.0

            def row(r):
                here8 = pl.multiple_of(r * 8, 8)
                back8 = pl.multiple_of((r - 1) * 8, 8)
                ats = [(row_tile(r, g), row_tile(r + 1, g), row_tile(r - 1, g)) for g in range(GROUPS)]
                near, far, last = [], [], []
                for at, _, _ in ats:
                    v = src[at, cols_of(0)]
                    near.append((v, pltpu.roll(v, 1, 1), pltpu.roll(v, 127, 1)))
                    last.append(pltpu.roll(src[at, cols_of(TILES - 1)], 1, 1))
                first_east = [x[2] for x in near]
                for j in range(TILES):
                    cols = cols_of(j)
                    here, back = pl.ds(here8, 8), pl.ds(back8, 8)
                    ck, ce, cw = k_ref[here, cols], e_ref[here, cols], w_ref[here, cols]
                    cn, cs = n_ref[here, cols], n_ref[back, cols]
                    for g, (at, over, under) in enumerate(ats):
                        v, west, east = near[g]
                        if j < TILES - 1:
                            ahead = src[at, cols_of(j + 1)]
                            following = (ahead, pltpu.roll(ahead, 1, 1), pltpu.roll(ahead, 127, 1))
                            next_east = following[2]
                        else:
                            following, next_east = None, first_east[g]
                        total = (
                            ck * v
                            + ce * jnp.where(is_last, next_east, east)
                            + cw * jnp.where(is_first, last[g], west)
                            + cn * src[over, cols]
                            + cs * src[under, cols]
                        )
                        dst[at, cols] = jnp.where(keep, total, v)
                        near[g], last[g] = following, west

            row(first)
            row(second)

        def across(k, low, high):
            def pair(i, _):
                passing(k, low + 2 * i, low + 2 * i + 1)
                return 0

            lax.fori_loop(0, (high - low) // 2, pair, 0)

        return passing, across

    def localize_pass(result, k):
        localization(result)[1](k, 1 + k, EXT - 1 - k)

    def localize(result):
        for k in range(PASSES):
            localize_pass(result, k)

    def localize_stage(result, stage):
        passing, across = localization(result)
        for k in range(stage):
            dist = stage - 1 - k
            if dist:
                passing(k, below_row(dist), above_row(dist))
            else:
                across(k, HALO, HALO + ROWS)


    col_iota = lax.broadcasted_iota(jnp.int32, (256, 128), 0).astype(F32).astype(BF16)
    ones, zeros = jnp.ones((256, 128), BF16), jnp.zeros((256, 128), BF16)

    def build_one_hots():
        mem_wait(IDS)
        ids = mr_ref[IDS].reshape(DEVS, DEVS).T
        rf_all = jnp.floor(ids * (1.0 / 256.0))
        rf_ref[...] = rf_all.astype(jnp.int32)
        ct_ref[...] = ids - rf_all * 256.0

        def build(b, _):
            cols = ct_ref[pl.ds(pl.multiple_of(b * SLOTS, SLOTS), SLOTS), :]
            for s in range(SLOTS):
                same = jnp.broadcast_to(cols[s : s + 1, :], (16, 128)).astype(BF16)
                same = jnp.concatenate([same] * 16, axis=0)
                oh_ref[b, :, s * 128 : (s + 1) * 128] = jnp.where(col_iota == same, ones, zeros)
            return 0

        lax.fori_loop(0, NM, build, 0)

    row_key = lax.broadcasted_iota(jnp.int32, (64, 128), 0)
    key = (row_key // 8) * FIELDS + lax.rem(row_key, 4)
    is_high = lax.rem(row_key, 8) < 4

    def window(b):
        start = BLOCK * b
        first = (start // 128) * 128
        return first, start - first

    for iteration in range(ITERS):
        base = 1 + 3 * iteration
        PICK, WGT, SUM = base, base + 1, base + 2
        if iteration == 0:
            for stage in range(1, HALO + 1):
                halo_take(DIR, stage, x_ref)
                localize_stage(l0_ref, stage)
                if stage == 3:
                    tile_wait(IDS)
                    ms_ref[IDS, 0] = tile_table(IDS)
                    mem_start(IDS, False)
            build_one_hots()

        def partial(r, _):
            total = zero_tile
            for g in range(GROUPS):
                at = row_tile(r + HALO, g)
                field = l0_ref[at, :]
                if iteration:
                    field = lr_ref[at, :] - first_step * z_ref[at, :] + beta * field
                total = total + em_ref[at, :] * field.astype(BF16).astype(F32)
            total = total + pltpu.roll(total, 4, 0)
            high, low = split(total)
            adj_ref[pl.ds(pl.multiple_of(r * 8, 8), 8), :] = jnp.where(low_half, high, low)
            return 0

        lax.fori_loop(0, ROWS, partial, 0)
        for b in range(NM):
            first, shift = window(b)
            piece = adj_ref[:, first : first + 384]
            if shift:
                piece = pltpu.roll(piece, 384 - shift, 1)
            lb_ref[b] = piece[:, :256].astype(BF16)

        def gather(b, _):
            got = jnp.dot(lb_ref[b], oh_ref[b], preferred_element_type=F32)
            rows16 = pl.ds(pl.multiple_of(b * SLOTS, SLOTS), SLOTS)
            wanted = rf_ref[rows16, :]
            rows = []
            for s in range(SLOTS):
                part = jnp.where(
                    key == wanted[s : s + 1, :], got[:, s * 128 : (s + 1) * 128], 0.0
                )
                rows.append(jnp.sum(part, axis=0, keepdims=True))
            pk_ref[rows16, :] = jnp.concatenate(rows, axis=0)
            return 0

        lax.fori_loop(0, NM, gather, 0)
        ms_ref[PICK] = pk_ref[...].T.reshape(NM, NT, 128)
        mem_start(PICK, True)
        if iteration == 0:
            x_ref[pl.ds(OWN, ROWS * PAD), :] = lr_ref[pl.ds(OWN, ROWS * PAD), :]
            for dist in range(1, HALO + 1):
                halo_take(RES, dist, x_ref)
            localize_pass(lr_ref, 0)
        else:

            def turn(r, _):
                for g in range(GROUPS):
                    at = row_tile(r + HALO, g)
                    res = r_ref[at, :] - first_step * im_ref[at, :]
                    r_ref[at, :] = res
                    d_ref[at, :] = res + beta * d_ref[at, :]
                return 0

            lax.fori_loop(0, ROWS, turn, 0)
        mem_wait(PICK)
        summed = mr_ref[PICK, 0]
        for k in range(1, NM):
            summed = summed + mr_ref[PICK, k]
        tile_rows(PICK, summed * weight)
        tile_start(PICK, True)
        if iteration == 0:
            localize_pass(lr_ref, 1)
        else:
            loaded("sol")
            for p in range(PLANES):
                out_sol[p] = sol_ref[p] + first_step * dir_ref[p]
        tile_wait(PICK)

        high, low = split(tile_table(PICK))
        both = jnp.concatenate([high, low], axis=0).astype(BF16)
        seen = jnp.dot(both, one_q[...], preferred_element_type=F32)
        value = jnp.sum(seen * one_t[...], axis=0, keepdims=True)
        u = value * inv_err
        along = lax.broadcasted_iota(jnp.int32, (1, SEGMENT), 1)
        following = jnp.where(along == SEGMENT - 1, 0.0, pltpu.roll(u, SEGMENT - 1, 1))
        preceding = jnp.where(along == 0, 0.0, pltpu.roll(u, 1, 1))
        ends = ((along == 0) | (along == SEGMENT - 1)).astype(F32)
        square = CORRELATION * CORRELATION
        mixed = ((1.0 + square - square * ends) * u - CORRELATION * (following + preceding)) / (
            1.0 - square
        )
        weighted = mixed * inv_err
        high, low = split(weighted)
        table = to_table(high, low)
        tile_rows(WGT, table[:NT] + table[NT:])
        tile_start(WGT, True)
        if iteration == 0:
            localize_pass(lr_ref, 2)
        tile_wait(WGT)
        ms_ref[WGT, 0] = tile_table(WGT)
        mem_start(WGT, False)
        if iteration == 0:
            localize_pass(lr_ref, 3)
        mem_wait(WGT)
        pk_ref[...] = mr_ref[WGT].reshape(DEVS, DEVS).T

        def scatter(b, _):
            rows16 = pl.ds(pl.multiple_of(b * SLOTS, SLOTS), SLOTS)
            wanted = rf_ref[rows16, :]
            high, low = split(pk_ref[rows16, :])
            parts = []
            for s in range(SLOTS):
                row = jnp.where(is_high, high[s : s + 1, :], low[s : s + 1, :])
                parts.append(jnp.where(key == wanted[s : s + 1, :], row, 0.0).astype(BF16))
            ob_ref[b] = lax.dot_general(
                jnp.concatenate(parts, axis=1),
                oh_ref[b],
                (((1,), (1,)), ((), ())),
                preferred_element_type=F32,
            )
            return 0

        lax.fori_loop(0, NM, scatter, 0)
        adj_ref[...] = jnp.zeros((64, WIDE), F32)
        for b in range(NM):
            first, shift = window(b)
            piece = jnp.concatenate([ob_ref[b], jnp.zeros((64, 128), F32)], axis=1)
            if shift:
                piece = pltpu.roll(piece, shift, 1)
            adj_ref[:, first : first + 384] = adj_ref[:, first : first + 384] + piece
        lane64 = lax.broadcasted_iota(jnp.int32, (64, 128), 1)
        head, tail = adj_ref[:, 0:128], adj_ref[:, WIDE - 128 : WIDE]
        adj_ref[:, WIDE - 128 : WIDE] = jnp.where(
            lane64 < 32, tail, jnp.where(lane64 < 96, pltpu.roll(head, 32, 1), pltpu.roll(tail, 96, 1))
        )
        own_rows = []
        for i in range(ROWS):
            tile = adj_ref[pl.ds(i * 8, 8), :]
            tile = (tile + pltpu.roll(tile, 4, 0)) * weight
            ax_ref[pl.ds((HALO + i) * 8, 8), :] = tile
        for side in range(2):
            tiles = []
            for i in range(HALO // 2):
                first = HALO + HALO * side + 2 * i
                tiles.append(
                    jnp.where(
                        low_half,
                        ax_ref[pl.ds(first * 8, 8), :],
                        ax_ref[pl.ds((first + 1) * 8, 8), :],
                    )
                )
            as_ref[iteration, side] = jnp.concatenate(tiles, axis=0).astype(BF16)
        sides_start(*edges, iteration)
        if iteration == 0:
            for dist in range(1, HALO + 1):
                halo_take(ENS, dist, em_ref)
        sides_wait(*edges, iteration)
        for side in range(2):
            arrived = ar_ref[iteration, side].astype(F32)
            for i in range(HALO // 2):
                first = (HALO + ROWS) * side + 2 * i
                packed = arrived[i * 8 : (i + 1) * 8, :]
                turned = pltpu.roll(packed, 4, 0)
                ax_ref[pl.ds(first * 8, 8), :] = jnp.where(low_half, packed, turned)
                ax_ref[pl.ds((first + 1) * 8, 8), :] = jnp.where(low_half, turned, packed)

        def back(r, _):
            row = ax_ref[pl.ds(pl.multiple_of(r * 8, 8), 8), :]
            for g in range(GROUPS):
                at = row_tile(r, g)
                x_ref[at, :] = (em_ref[at, :] * row).astype(BF16).astype(F32)
            return 0

        lax.fori_loop(0, EXT, back, 0)
        localize(z_ref)

        def image(r, carry):
            sea_row = s_ref[pl.ds(pl.multiple_of(r * 8, 8), 8), :]
            sums = list(carry)
            for g in range(GROUPS):
                at = row_tile(r + HALO, g)
                d, res = d_ref[at, :], r_ref[at, :]
                moved = sea_row * z_ref[at, :]
                img = d + moved
                im_ref[at, :] = img
                if iteration == 0:
                    x_ref[at, :] = img * sea_row
                terms = [d * img, res * res]
                if iteration == 0:
                    terms += [res * img, img * img]
                sums = [total + fold(term, valid) for total, term in zip(sums, terms)]
            return tuple(sums)

        count_sums = 4 if iteration == 0 else 2
        sums = lax.fori_loop(0, ROWS, image, (jnp.zeros((8, 128), F32),) * count_sums)
        packed = jnp.zeros((8, 128), F32)
        for i, total in enumerate(sums):
            packed = jnp.where(sub_small == i, jnp.sum(total, axis=0, keepdims=True), packed)
        ts_ref[SUM, 0] = packed
        tile_start(SUM, False)
        if iteration == 0:
            for dist in range(1, HALO + 1):
                halo_send(IMG, dist, masked(x_ref))
            halo_take(IMG, 1, x_ref)
            localize_stage(z_ref, 1)
        else:
            for g in range(GROUPS):
                d = planes_first(d_ref, g)
                res = planes_first(r_ref, g)
                img = planes_first(im_ref, g)
                for i in range(min(8, PLANES - 8 * g)):
                    p = 8 * g + i
                    dir_ref[p] = d[i]
                    out_res[p] = res[i]
                    res_ref[p] = img[i]
        tile_wait(SUM)
        part = tr_ref[SUM, 0]
        for k in range(1, NT):
            part = part + tr_ref[SUM, k]
        ms_ref[SUM, 0, pl.ds(0, 8), :] = part
        ms_ref[SUM, 0, pl.ds(8, 8), :] = part
        mem_start(SUM, False)
        if iteration == 0:
            for stage in range(2, HALO + 1):
                halo_take(IMG, stage, x_ref)
                localize_stage(z_ref, stage)
        mem_wait(SUM)
        total = mr_ref[SUM, 0, pl.ds(0, 8), :]
        for k in range(1, NM):
            total = total + mr_ref[SUM, k, pl.ds(0, 8), :]
        total = jnp.sum(total, axis=1, keepdims=True)
        d_image, rr = total[0:1, :], total[1:2, :]
        step = rr / d_image
        if iteration == 0:
            r_image, image_image = total[2:3, :], total[3:4, :]
            fresh = rr - 2.0 * step * r_image + step * step * image_image
            beta = fresh / rr
            first_step = step
        else:
            for p in range(PLANES):
                out_sol[p] = out_sol[p] + step * dir_ref[p]
                out_res[p] = out_res[p] - step * res_ref[p]

    for i in range(1 + 3 * ITERS):
        ref = mr_ref.at[i, pl.ds(0, NM - 1)]
        pltpu.make_async_copy(ref, ref, m_send.at[i]).wait()
        ref = tr_ref.at[i, pl.ds(0, NT - 1)]
        pltpu.make_async_copy(ref, ref, t_send.at[i]).wait()
    for kind in range(4):
        for dist in range(1, HALO + 1):
            for copy in halo_piece(kind, dist):
                copy.wait_send()
    for group, many in ((edges, ITERS), (faces, 1)):
        for i in range(many):
            for copy in sides(*group, i):
                copy.wait_send()


def shards(
    solution,
    residual,
    direction,
    ensemble,
    east_rate,
    north_rate,
    sea_mask,
    pass_counts,
    obs_owner,
    obs_cell,
    obs_level,
    obs_variable,
    obs_error,
):
    def planes(x):
        return x.reshape(PLANES, ROWS, LONS)

    def row(x):
        return x.reshape(1, SEGMENT)

    exchanges = 1 + 3 * ITERS
    vmem = pl.BlockSpec(memory_space=pltpu.VMEM)
    hbm = pl.BlockSpec(memory_space=pltpu.HBM)
    planes_f32 = pltpu.VMEM((PLANES, ROWS, LONS), F32)
    row_i32 = pltpu.VMEM((1, SEGMENT), jnp.int32)
    field = pltpu.VMEM((EXT * PAD, WIDE), F32)
    band = pltpu.VMEM((EXT * 8, WIDE), F32)
    shape = jax.ShapeDtypeStruct((PLANES, ROWS, LONS), F32)
    sol, res = pl.pallas_call(
        body,
        out_shape=(shape, shape),
        in_specs=[hbm] * 7 + [pl.BlockSpec(memory_space=pltpu.SMEM)] + [hbm] * 5,
        out_specs=(vmem, vmem),
        scratch_shapes=[
            planes_f32,
            planes_f32,
            planes_f32,
            pltpu.VMEM((PLANES, ROWS, LONS), BF16),
            pltpu.VMEM((ROWS, LONS), F32),
            pltpu.VMEM((ROWS, LONS), F32),
            pltpu.VMEM((ROWS, LONS), jnp.int32),
            row_i32,
            row_i32,
            row_i32,
            row_i32,
            pltpu.VMEM((1, SEGMENT), F32),
            pltpu.SemaphoreType.DMA((12,)),
            field,
            field,
            field,
            field,
            field,
            field,
            field,
            field,
            field,
            field,
            field,
            band,
            band,
            band,
            band,
            pltpu.VMEM((ROWS * 8, WIDE), F32),
            pltpu.VMEM((NM, 64, 256), BF16),
            pltpu.VMEM((NM, 256, SLOTS * 128), BF16),
            pltpu.VMEM((DEVS, 128), jnp.int32),
            pltpu.VMEM((DEVS, 128), F32),
            pltpu.VMEM((DEVS, 128), F32),
            pltpu.VMEM((NM, 64, 256), F32),
            pltpu.VMEM((64, WIDE), F32),
            band,
            pltpu.VMEM((DEVS, SEGMENT), BF16),
            pltpu.VMEM((2 * NT, SEGMENT), F32),
            pltpu.VMEM((PASSES, 8, 128), F32),
            pltpu.VMEM((4, 2, HALO, PAD, WIDE), BF16),
            pltpu.VMEM((4, 2, HALO, PAD, WIDE), BF16),
            pltpu.VMEM((ITERS, 2, 16, WIDE), BF16),
            pltpu.VMEM((ITERS, 2, 16, WIDE), BF16),
            pltpu.VMEM((1, 2, 8, WIDE), F32),
            pltpu.VMEM((1, 2, 8, WIDE), F32),
            pltpu.VMEM((exchanges, NM, NT, 128), F32),
            pltpu.VMEM((exchanges, NM, NT, 128), F32),
            pltpu.VMEM((exchanges, NT, 8, 128), F32),
            pltpu.VMEM((exchanges, NT, 8, 128), F32),
            pltpu.SemaphoreType.DMA((4, HALO, 2)),
            pltpu.SemaphoreType.DMA((4, HALO, 2)),
            pltpu.SemaphoreType.DMA((ITERS, 2)),
            pltpu.SemaphoreType.DMA((ITERS, 2)),
            pltpu.SemaphoreType.DMA((1, 2)),
            pltpu.SemaphoreType.DMA((1, 2)),
            pltpu.SemaphoreType.DMA((exchanges,)),
            pltpu.SemaphoreType.DMA((exchanges,)),
            pltpu.SemaphoreType.DMA((exchanges,)),
            pltpu.SemaphoreType.DMA((exchanges,)),
        ],
        compiler_params=pltpu.CompilerParams(
            collective_id=0, has_side_effects=True, vmem_limit_bytes=LIMIT
        ),
    )(
        planes(direction),
        planes(residual),
        planes(solution),
        planes(ensemble),
        east_rate,
        north_rate,
        sea_mask,
        pass_counts,
        row(obs_owner),
        row(obs_cell),
        row(obs_level),
        row(obs_variable),
        row(obs_error),
    )
    return sol.reshape(solution.shape), res.reshape(solution.shape)


def solution(mesh):
    return jax.shard_map(
        shards,
        mesh=mesh,
        in_specs=(
            P("mem", None, "tile", None),
            P("mem", None, "tile", None),
            P("mem", None, "tile", None),
            P("mem", None, "tile", None),
            P("tile", None),
            P("tile", None),
            P("tile", None),
            P(),
            P(("mem", "tile"), None),
            P(("mem", "tile")),
            P(("mem", "tile")),
            P(("mem", "tile")),
            P(("mem", "tile")),
        ),
        out_specs=(P("mem", None, "tile", None), P("mem", None, "tile", None)),
        check_vma=False,
    )
```

```python
import functools
import math

import jax
import jax.numpy as jnp
from jax import lax
from jax.experimental import pallas as pl
from jax.experimental.pallas import tpu as pltpu
from jax.sharding import PartitionSpec as P

MESH = pl.DeviceIdType.MESH
F32 = jnp.float32
BF16 = jnp.bfloat16

FIELDS = 4
LEVELS = 2
PASSES = 4
ITERS = 2
CORRELATION = 0.6
MEMBERS_DEV = 5
MEMBERS = 40
ROWS = 8
LONS = 1440
BLOCK = 180
SLOTS = 16
SEGMENT = 1024
NM = 8
NT = 16

HALO = 4
EXT = ROWS + 2 * HALO
PLANES = MEMBERS_DEV * FIELDS
PAD = 24
GROUPS = PAD // 8
WIDE = 1536
OWN = HALO * PAD
EDGE = HALO * PAD
DEVS = NM * NT
LIMIT = 60 * 1024 * 1024
TILES = WIDE // 128

IDS = 0


def widen(x):
    return jnp.concatenate([x, x[:, :64], x[:, 1408:1440]], axis=1)


def split(x):
    high = x.astype(BF16).astype(F32)
    return high, x - high


def fold(x, valid):
    total = x[:, 0:128]
    for k in range(1, WIDE // 128 - 1):
        total = total + x[:, 128 * k : 128 * (k + 1)]
    return total + x[:, WIDE - 128 : WIDE] * valid


def cols_of(j):
    return slice(128 * j, 128 * (j + 1))


def row_tile(r, g=0):
    return pl.ds(pl.multiple_of(r * PAD + g * 8, 8), 8)


def body(
    dir_hbm,
    res_hbm,
    sol_hbm,
    ens_hbm,
    east_hbm,
    north_hbm,
    sea_hbm,
    counts_ref,
    owner_hbm,
    cell_hbm,
    level_hbm,
    variable_hbm,
    error_hbm,
    out_sol,
    out_res,
    dir_ref,
    res_ref,
    sol_ref,
    ens_ref,
    east_ref,
    north_ref,
    sea_ref,
    owner_ref,
    cell_ref,
    level_ref,
    variable_ref,
    error_ref,
    load_sem,
    d_ref,
    r_ref,
    im_ref,
    x_ref,
    p1_ref,
    p2_ref,
    p3_ref,
    z_ref,
    l0_ref,
    lr_ref,
    em_ref,
    e_ref,
    n_ref,
    w_ref,
    k_ref,
    s_ref,
    lb_ref,
    oh_ref,
    rf_ref,
    ct_ref,
    pk_ref,
    ob_ref,
    adj_ref,
    ax_ref,
    one_q,
    one_t,
    pass_ref,
    hs_ref,
    hr_ref,
    as_ref,
    ar_ref,
    cs_ref,
    cr_ref,
    ms_ref,
    mr_ref,
    ts_ref,
    tr_ref,
    h_send,
    h_recv,
    a_send,
    a_recv,
    c_send,
    c_recv,
    m_send,
    m_recv,
    t_send,
    t_recv,
):
    m = lax.axis_index("mem")
    t = lax.axis_index("tile")
    up = lax.rem(t + 1, NT)
    down = lax.rem(t + NT - 1, NT)
    weight = 1.0 / math.sqrt(MEMBERS - 1)

    loads = {}
    for i, (name, source, target) in enumerate(
        (
            ("dir", dir_hbm, dir_ref),
            ("sea", sea_hbm, sea_ref),
            ("east", east_hbm, east_ref),
            ("north", north_hbm, north_ref),
            ("owner", owner_hbm, owner_ref),
            ("cell", cell_hbm, cell_ref),
            ("level", level_hbm, level_ref),
            ("variable", variable_hbm, variable_ref),
            ("error", error_hbm, error_ref),
            ("ens", ens_hbm, ens_ref),
            ("res", res_hbm, res_ref),
            ("sol", sol_hbm, sol_ref),
        )
    ):
        loads[name] = pltpu.make_async_copy(source, target, load_sem.at[i])
        loads[name].start()

    def loaded(*which):
        for name in which:
            loads[name].wait()

    barrier = pltpu.get_barrier_semaphore()

    def greet_mem(k, _):
        pl.semaphore_signal(
            barrier, inc=1, device_id=(lax.rem(m + k, NM), t), device_id_type=MESH
        )
        return 0

    def greet_tile(k, _):
        pl.semaphore_signal(
            barrier, inc=1, device_id=(m, lax.rem(t + k, NT)), device_id_type=MESH
        )
        return 0

    lax.fori_loop(1, NM, greet_mem, 0)
    lax.fori_loop(1, NT, greet_tile, 0)

    def mem_start(i, pick):
        def one(k, _):
            peer = lax.rem(m + k, NM)
            pltpu.make_async_remote_copy(
                src_ref=ms_ref.at[i, peer if pick else 0],
                dst_ref=mr_ref.at[i, m],
                send_sem=m_send.at[i],
                recv_sem=m_recv.at[i],
                device_id=(peer, t),
                device_id_type=MESH,
            ).start()
            return 0

        lax.fori_loop(1, NM, one, 0)
        mr_ref[i, m] = ms_ref[i, m if pick else 0]

    def mem_wait(i):
        ref = mr_ref.at[i, pl.ds(0, NM - 1)]
        pltpu.make_async_copy(ref, ref, m_recv.at[i]).wait()

    def tile_start(i, pick):
        def one(k, _):
            peer = lax.rem(t + k, NT)
            pltpu.make_async_remote_copy(
                src_ref=ts_ref.at[i, peer if pick else 0],
                dst_ref=tr_ref.at[i, t],
                send_sem=t_send.at[i],
                recv_sem=t_recv.at[i],
                device_id=(m, peer),
                device_id_type=MESH,
            ).start()
            return 0

        lax.fori_loop(1, NT, one, 0)
        tr_ref[i, t] = ts_ref[i, t if pick else 0]

    def tile_wait(i):
        ref = tr_ref.at[i, pl.ds(0, NT - 1)]
        pltpu.make_async_copy(ref, ref, t_recv.at[i]).wait()

    def sides(send, recv, ssem, rsem, i):
        low = pltpu.make_async_remote_copy(
            src_ref=send.at[i, 0],
            dst_ref=recv.at[i, 1],
            send_sem=ssem.at[i, 0],
            recv_sem=rsem.at[i, 1],
            device_id=(m, down),
            device_id_type=MESH,
        )
        high = pltpu.make_async_remote_copy(
            src_ref=send.at[i, 1],
            dst_ref=recv.at[i, 0],
            send_sem=ssem.at[i, 1],
            recv_sem=rsem.at[i, 0],
            device_id=(m, up),
            device_id_type=MESH,
        )
        return low, high

    def sides_start(*which):
        for copy in sides(*which):
            copy.start()

    def sides_wait(*which):
        for copy in sides(*which):
            copy.wait_recv()

    edges = (as_ref, ar_ref, a_send, a_recv)
    faces = (cs_ref, cr_ref, c_send, c_recv)
    DIR, ENS, RES, IMG = 0, 1, 2, 3

    def halo_piece(kind, dist):
        low = pltpu.make_async_remote_copy(
            src_ref=hs_ref.at[kind, 0, dist - 1],
            dst_ref=hr_ref.at[kind, 1, dist - 1],
            send_sem=h_send.at[kind, dist - 1, 0],
            recv_sem=h_recv.at[kind, dist - 1, 1],
            device_id=(m, down),
            device_id_type=MESH,
        )
        high = pltpu.make_async_remote_copy(
            src_ref=hs_ref.at[kind, 1, dist - 1],
            dst_ref=hr_ref.at[kind, 0, dist - 1],
            send_sem=h_send.at[kind, dist - 1, 1],
            recv_sem=h_recv.at[kind, dist - 1, 0],
            device_id=(m, up),
            device_id_type=MESH,
        )
        return low, high

    def below_row(dist):
        return HALO - dist

    def above_row(dist):
        return HALO + ROWS - 1 + dist

    def whole_row(r):
        return pl.ds(r * PAD, PAD)

    def halo_send(kind, dist, row_of):
        hs_ref[kind, 0, dist - 1] = row_of(HALO + dist - 1).astype(BF16)
        hs_ref[kind, 1, dist - 1] = row_of(HALO + ROWS - dist).astype(BF16)
        for copy in halo_piece(kind, dist):
            copy.start()

    def halo_take(kind, dist, dst):
        for copy in halo_piece(kind, dist):
            copy.wait_recv()
        dst[whole_row(below_row(dist)), :] = hr_ref[kind, 0, dist - 1].astype(F32)
        dst[whole_row(above_row(dist)), :] = hr_ref[kind, 1, dist - 1].astype(F32)

    sub = lax.broadcasted_iota(jnp.int32, (8, WIDE), 0)
    lane = lax.broadcasted_iota(jnp.int32, (8, 128), 1)
    valid = (lane < LONS - (WIDE - 128)).astype(F32)
    sub_small = lax.broadcasted_iota(jnp.int32, (8, 128), 0)
    low_half = sub < 4
    is_first, is_last = lane == 0, lane == 127

    loaded("sea", "east", "north")
    sea = widen(sea_ref[...].astype(F32))
    east = widen(east_ref[...])
    north = widen(north_ref[...])
    sea_up = pltpu.roll(sea, 7, 0)
    east_face = east * sea * pltpu.roll(sea, WIDE - 1, 1)
    north_raw = north * sea
    north_face = jnp.where(sub < 7, north_raw * sea_up, north_raw)
    cs_ref[0, 1] = jnp.where(low_half, pltpu.roll(east_face, 4, 0), north_face)
    cs_ref[0, 0] = jnp.where(
        low_half, east_face, jnp.where(sub < 7, pltpu.roll(north_face, 4, 0), sea_up)
    )

    def spread_row(value, i):
        return jnp.broadcast_to(value[i : i + 1, :], (8, WIDE))

    for i in range(ROWS):
        e_ref[pl.ds((HALO + i) * 8, 8), :] = spread_row(east_face, i)
        n_ref[pl.ds((HALO + i) * 8, 8), :] = spread_row(north_face, i)
        s_ref[pl.ds(i * 8, 8), :] = spread_row(sea, i)

    field_of = lax.rem(sub_small, 4)
    c0, c1, c2, c3 = (counts_ref[0], counts_ref[1], counts_ref[2], counts_ref[3])
    count = jnp.where(
        field_of == 0, c0, jnp.where(field_of == 1, c1, jnp.where(field_of == 2, c2, c3))
    )
    for k in range(PASSES):
        pass_ref[k] = (count > k).astype(F32)

    zero_tile = jnp.zeros((8, WIDE), F32)

    def rows_first(ref, g):
        parts = [widen(ref[8 * g + i].astype(F32)) for i in range(min(8, PLANES - 8 * g))]
        parts += [zero_tile] * (8 - len(parts))
        return jnp.stack(parts, axis=0).transpose(1, 0, 2)

    def planes_first(ref, g):
        rows = jnp.stack([ref[row_tile(HALO + i, g), :] for i in range(ROWS)], axis=0)
        return rows.transpose(1, 0, 2)[:, :, :LONS]

    def sea_rows(r):
        return s_ref[pl.ds(pl.multiple_of(r * 8, 8), 8), :]

    loaded("dir")
    for g in range(GROUPS):
        turned = rows_first(dir_ref, g)
        for i in range(ROWS):
            d_ref[row_tile(HALO + i, g), :] = turned[i]
            x_ref[row_tile(HALO + i, g), :] = turned[i] * sea_rows(i)

    pl.semaphore_wait(barrier, NM + NT - 2)

    sides_start(*faces, 0)

    def masked(ref):
        return lambda r: ref[whole_row(r), :]

    halo_send(DIR, 1, masked(x_ref))
    halo_send(DIR, 2, masked(x_ref))

    loaded("owner", "cell", "level", "variable", "error")
    owner = owner_ref[...]
    cell = cell_ref[...].astype(F32)
    cell_row = jnp.floor((cell + 0.5) * (1.0 / BLOCK))
    col_id = cell - cell_row * BLOCK
    rf_id = cell_row * FIELDS + (variable_ref[...] * LEVELS + level_ref[...]).astype(F32)
    inv_err = 1.0 / error_ref[...]
    owner_tile = lax.rem(owner, NT)
    owner_mem = owner // NT
    dev_iota = lax.broadcasted_iota(jnp.int32, (DEVS, SEGMENT), 0)
    owns = jnp.where(dev_iota == owner, 1.0, 0.0)
    before = jnp.where(
        lax.broadcasted_iota(jnp.int32, (SEGMENT, SEGMENT), 0)
        < lax.broadcasted_iota(jnp.int32, (SEGMENT, SEGMENT), 1),
        1.0,
        0.0,
    ).astype(BF16)
    ranks = jnp.dot(owns.astype(BF16), before, preferred_element_type=F32)
    slot = jnp.sum(ranks * owns, axis=0, keepdims=True).astype(jnp.int32)
    place = owner_mem * SLOTS + slot
    one_q[...] = jnp.where(dev_iota == place, 1.0, 0.0).astype(BF16)
    t_iota = lax.rem(lax.broadcasted_iota(jnp.int32, (2 * NT, SEGMENT), 0), NT)
    t_is_high = lax.broadcasted_iota(jnp.int32, (2 * NT, SEGMENT), 0) < NT
    one_t[...] = jnp.where(t_iota == owner_tile, 1.0, 0.0)

    def to_table(high, low):
        left = one_t[...] * jnp.where(t_is_high, high, low)
        return lax.dot_general(
            left.astype(BF16), one_q[...], (((1,), (1,)), ((), ())), preferred_element_type=F32
        )

    def tile_rows(i, table):
        for k in range(NT):
            ts_ref[i, k] = table[k : k + 1, :]

    def tile_table(i):
        return jnp.concatenate([tr_ref[i, k] for k in range(NT)], axis=0)

    table = to_table(col_id, rf_id)
    tile_rows(IDS, table[NT:] * 256.0 + table[:NT])

    tile_start(IDS, True)
    halo_send(DIR, 3, masked(x_ref))
    halo_send(DIR, 4, masked(x_ref))

    loaded("res")
    for g in range(GROUPS):
        turned = rows_first(res_ref, g)
        for i in range(ROWS):
            r_ref[row_tile(HALO + i, g), :] = turned[i]
            lr_ref[row_tile(HALO + i, g), :] = turned[i] * sea_rows(i)
    for dist in range(1, HALO + 1):
        halo_send(RES, dist, masked(lr_ref))

    loaded("ens")
    for g in range(GROUPS):
        turned = rows_first(ens_ref, g)
        for i in range(ROWS):
            em_ref[row_tile(HALO + i, g), :] = turned[i] * sea_rows(i)

    sides_wait(*faces, 0)
    below, above = cr_ref[0, 0], cr_ref[0, 1]
    not_first = jnp.where(t > 0, 1.0, 0.0)
    not_last = jnp.where(t < NT - 1, 1.0, 0.0)
    for i in range(HALO):
        e_ref[pl.ds(i * 8, 8), :] = spread_row(below, i)
        e_ref[pl.ds((HALO + ROWS + i) * 8, 8), :] = spread_row(above, i)
    for i in range(HALO - 1):
        n_ref[pl.ds(i * 8, 8), :] = spread_row(below, HALO + i)
        n_ref[pl.ds((HALO + ROWS + i) * 8, 8), :] = spread_row(above, HALO + i)
    n_ref[pl.ds((HALO - 1) * 8, 8), :] = (
        spread_row(below, 2 * HALO - 1) * s_ref[pl.ds(0, 8), :] * not_first
    )
    n_ref[pl.ds((HALO + ROWS - 1) * 8, 8), :] = (
        n_ref[pl.ds((HALO + ROWS - 1) * 8, 8), :] * spread_row(above, 2 * HALO - 1) * not_last
    )

    for r in range(1, EXT - 1):
        here = pl.ds(r * 8, 8)
        e, n, s = e_ref[here, :], n_ref[here, :], n_ref[pl.ds((r - 1) * 8, 8), :]
        w = pltpu.roll(e, 1, 1)
        w_ref[here, :] = w
        k_ref[here, :] = 1.0 - e - w - n - s

    levels = (x_ref, p1_ref, p2_ref, p3_ref)

    def localization(result):
        def passing(k, *rows):
            src = levels[k]
            dst = levels[k + 1] if k + 1 < PASSES else result
            keep = jnp.broadcast_to(pass_ref[k][:, 0:1], (8, 128)) > 0.0

            def row(r):
                here8 = pl.multiple_of(r * 8, 8)
                back8 = pl.multiple_of((r - 1) * 8, 8)
                ats = [(row_tile(r, g), row_tile(r + 1, g), row_tile(r - 1, g)) for g in range(GROUPS)]
                near, far, last = [], [], []
                for at, _, _ in ats:
                    v = src[at, cols_of(0)]
                    near.append((v, pltpu.roll(v, 1, 1), pltpu.roll(v, 127, 1)))
                    last.append(pltpu.roll(src[at, cols_of(TILES - 1)], 1, 1))
                first_east = [x[2] for x in near]
                for j in range(TILES):
                    cols = cols_of(j)
                    here, back = pl.ds(here8, 8), pl.ds(back8, 8)
                    ck, ce, cw = k_ref[here, cols], e_ref[here, cols], w_ref[here, cols]
                    cn, cs = n_ref[here, cols], n_ref[back, cols]
                    for g, (at, over, under) in enumerate(ats):
                        v, west, east = near[g]
                        if j < TILES - 1:
                            ahead = src[at, cols_of(j + 1)]
                            following = (ahead, pltpu.roll(ahead, 1, 1), pltpu.roll(ahead, 127, 1))
                            next_east = following[2]
                        else:
                            following, next_east = None, first_east[g]
                        total = (
                            ck * v
                            + ce * jnp.where(is_last, next_east, east)
                            + cw * jnp.where(is_first, last[g], west)
                            + cn * src[over, cols]
                            + cs * src[under, cols]
                        )
                        dst[at, cols] = jnp.where(keep, total, v)
                        near[g], last[g] = following, west

            for r in rows:
                row(r)

        def across(k, low, high):
            def quad(i, _):
                passing(k, *(low + 4 * i + j for j in range(4)))
                return 0

            whole = (high - low) // 4
            lax.fori_loop(0, whole, quad, 0)
            if low + 4 * whole < high:
                passing(k, *range(low + 4 * whole, high))

        return passing, across

    def localize_pass(result, k):
        localization(result)[1](k, 1 + k, EXT - 1 - k)

    def localize(result):
        for k in range(PASSES):
            localize_pass(result, k)

    def localize_stage(result, stage):
        passing, across = localization(result)
        for k in range(stage):
            dist = stage - 1 - k
            if dist:
                passing(k, below_row(dist), above_row(dist))
            else:
                across(k, HALO, HALO + ROWS)


    col_iota = lax.broadcasted_iota(jnp.int32, (256, 128), 0).astype(F32).astype(BF16)
    ones, zeros = jnp.ones((256, 128), BF16), jnp.zeros((256, 128), BF16)

    def build_one_hots():
        mem_wait(IDS)
        ids = mr_ref[IDS].reshape(DEVS, DEVS).T
        rf_all = jnp.floor(ids * (1.0 / 256.0))
        rf_ref[...] = rf_all.astype(jnp.int32)
        ct_ref[...] = ids - rf_all * 256.0

        def build(b, _):
            cols = ct_ref[pl.ds(pl.multiple_of(b * SLOTS, SLOTS), SLOTS), :]
            for s in range(SLOTS):
                same = jnp.broadcast_to(cols[s : s + 1, :], (16, 128)).astype(BF16)
                same = jnp.concatenate([same] * 16, axis=0)
                oh_ref[b, :, s * 128 : (s + 1) * 128] = jnp.where(col_iota == same, ones, zeros)
            return 0

        lax.fori_loop(0, NM, build, 0)

    row_key = lax.broadcasted_iota(jnp.int32, (64, 128), 0)
    key = (row_key // 8) * FIELDS + lax.rem(row_key, 4)
    is_high = lax.rem(row_key, 8) < 4

    def window(b):
        start = BLOCK * b
        first = (start // 128) * 128
        return first, start - first

    segment = lax.broadcasted_iota(jnp.int32, (1, 128), 1) // 32

    def sums_start(i, totals):
        packed = jnp.zeros((1, 128), F32)
        for k, total in enumerate(totals):
            total = jnp.sum(total, axis=0, keepdims=True)
            total = total + pltpu.roll(total, 64, 1)
            total = total + pltpu.roll(total, 32, 1)
            packed = jnp.where(segment == k, total, packed)
        ts_ref[i, 0] = packed
        tile_start(i, False)

    def sums_pass_on(i):
        tile_wait(i)
        part = tr_ref[i, 0]
        for k in range(1, NT):
            part = part + tr_ref[i, k]
        ms_ref[i, 0] = jnp.broadcast_to(part, (NT, 128))
        mem_start(i, False)

    def sums_get(i):
        mem_wait(i)
        total = mr_ref[i, 0, pl.ds(0, 8), :]
        for k in range(1, NM):
            total = total + mr_ref[i, k, pl.ds(0, 8), :]
        total = total[0:1, :]
        return [
            jnp.sum(jnp.where(segment == k, total, 0.0), axis=1, keepdims=True) for k in range(4)
        ]

    for iteration in range(ITERS):
        base = 1 + 3 * iteration
        PICK, WGT, SUM = base, base + 1, base + 2
        if iteration == 0:
            for stage in range(1, HALO + 1):
                halo_take(DIR, stage, x_ref)
                localize_stage(l0_ref, stage)
                if stage == 3:
                    tile_wait(IDS)
                    ms_ref[IDS, 0] = tile_table(IDS)
                    mem_start(IDS, False)
            build_one_hots()

        def partial(r, _):
            total = zero_tile
            for g in range(GROUPS):
                at = row_tile(r + HALO, g)
                field = l0_ref[at, :]
                if iteration:
                    field = lr_ref[at, :] - first_step * z_ref[at, :] + beta * field
                total = total + em_ref[at, :] * field.astype(BF16).astype(F32)
            total = total + pltpu.roll(total, 4, 0)
            high, low = split(total)
            adj_ref[pl.ds(pl.multiple_of(r * 8, 8), 8), :] = jnp.where(low_half, high, low)
            return 0

        lax.fori_loop(0, ROWS, partial, 0)
        for b in range(NM):
            first, shift = window(b)
            piece = adj_ref[:, first : first + 384]
            if shift:
                piece = pltpu.roll(piece, 384 - shift, 1)
            lb_ref[b] = piece[:, :256].astype(BF16)

        def gather(b, _):
            got = jnp.dot(lb_ref[b], oh_ref[b], preferred_element_type=F32)
            rows16 = pl.ds(pl.multiple_of(b * SLOTS, SLOTS), SLOTS)
            wanted = rf_ref[rows16, :]
            rows = []
            for s in range(SLOTS):
                part = jnp.where(
                    key == wanted[s : s + 1, :], got[:, s * 128 : (s + 1) * 128], 0.0
                )
                rows.append(jnp.sum(part, axis=0, keepdims=True))
            pk_ref[rows16, :] = jnp.concatenate(rows, axis=0)
            return 0

        lax.fori_loop(0, NM, gather, 0, unroll=2)
        ms_ref[PICK] = pk_ref[...].T.reshape(NM, NT, 128)
        mem_start(PICK, True)
        if iteration == 0:
            x_ref[pl.ds(OWN, ROWS * PAD), :] = lr_ref[pl.ds(OWN, ROWS * PAD), :]
            for dist in range(1, HALO + 1):
                halo_take(RES, dist, x_ref)
            localize_pass(lr_ref, 0)
        else:

            def turn(r, carry):
                rr, dd = carry
                for g in range(GROUPS):
                    at = row_tile(r + HALO, g)
                    res = r_ref[at, :] - first_step * im_ref[at, :]
                    d = res + beta * d_ref[at, :]
                    r_ref[at, :] = res
                    d_ref[at, :] = d
                    rr, dd = rr + fold(res * res, valid), dd + fold(d * d, valid)
                return rr, dd

            own_rr, own_dd = lax.fori_loop(0, ROWS, turn, (jnp.zeros((8, 128), F32),) * 2)
        mem_wait(PICK)
        summed = mr_ref[PICK, 0]
        for k in range(1, NM):
            summed = summed + mr_ref[PICK, k]
        tile_rows(PICK, summed * weight)
        tile_start(PICK, True)
        if iteration == 0:
            halo_send(ENS, 1, masked(em_ref))
            halo_send(ENS, 2, masked(em_ref))
            localize_pass(lr_ref, 1)
        else:
            loaded("sol")
            for p in range(PLANES):
                out_sol[p] = sol_ref[p] + first_step * dir_ref[p]
        tile_wait(PICK)

        high, low = split(tile_table(PICK))
        both = jnp.concatenate([high, low], axis=0).astype(BF16)
        seen = jnp.dot(both, one_q[...], preferred_element_type=F32)
        value = jnp.sum(seen * one_t[...], axis=0, keepdims=True)
        u = value * inv_err
        along = lax.broadcasted_iota(jnp.int32, (1, SEGMENT), 1)
        following = jnp.where(along == SEGMENT - 1, 0.0, pltpu.roll(u, SEGMENT - 1, 1))
        preceding = jnp.where(along == 0, 0.0, pltpu.roll(u, 1, 1))
        ends = ((along == 0) | (along == SEGMENT - 1)).astype(F32)
        square = CORRELATION * CORRELATION
        mixed = ((1.0 + square - square * ends) * u - CORRELATION * (following + preceding)) / (
            1.0 - square
        )
        weighted = mixed * inv_err
        high, low = split(weighted)
        table = to_table(high, low)
        tile_rows(WGT, table[:NT] + table[NT:])
        tile_start(WGT, True)
        if iteration == 0:
            halo_send(ENS, 3, masked(em_ref))
            halo_send(ENS, 4, masked(em_ref))
        else:
            product = value * weighted
            observed = product[:, 0:128]
            for k in range(1, SEGMENT // 128):
                observed = observed + product[:, 128 * k : 128 * (k + 1)]
            sums_start(SUM, (own_dd, own_rr, observed))
        if iteration == 0:
            localize_pass(lr_ref, 2)
        tile_wait(WGT)
        ms_ref[WGT, 0] = tile_table(WGT)
        mem_start(WGT, False)
        if iteration == 0:
            localize_pass(lr_ref, 3)
        else:
            sums_pass_on(SUM)
        mem_wait(WGT)
        pk_ref[...] = mr_ref[WGT].reshape(DEVS, DEVS).T

        def scatter(b, _):
            rows16 = pl.ds(pl.multiple_of(b * SLOTS, SLOTS), SLOTS)
            wanted = rf_ref[rows16, :]
            high, low = split(pk_ref[rows16, :])
            parts = []
            for s in range(SLOTS):
                row = jnp.where(is_high, high[s : s + 1, :], low[s : s + 1, :])
                parts.append(jnp.where(key == wanted[s : s + 1, :], row, 0.0).astype(BF16))
            ob_ref[b] = lax.dot_general(
                jnp.concatenate(parts, axis=1),
                oh_ref[b],
                (((1,), (1,)), ((), ())),
                preferred_element_type=F32,
            )
            return 0

        lax.fori_loop(0, NM, scatter, 0, unroll=2)
        adj_ref[...] = jnp.zeros((64, WIDE), F32)
        for b in range(NM):
            first, shift = window(b)
            piece = jnp.concatenate([ob_ref[b], jnp.zeros((64, 128), F32)], axis=1)
            if shift:
                piece = pltpu.roll(piece, shift, 1)
            adj_ref[:, first : first + 384] = adj_ref[:, first : first + 384] + piece
        lane64 = lax.broadcasted_iota(jnp.int32, (64, 128), 1)
        head, tail = adj_ref[:, 0:128], adj_ref[:, WIDE - 128 : WIDE]
        adj_ref[:, WIDE - 128 : WIDE] = jnp.where(
            lane64 < 32, tail, jnp.where(lane64 < 96, pltpu.roll(head, 32, 1), pltpu.roll(tail, 96, 1))
        )
        own_rows = []
        for i in range(ROWS):
            tile = adj_ref[pl.ds(i * 8, 8), :]
            tile = (tile + pltpu.roll(tile, 4, 0)) * weight
            ax_ref[pl.ds((HALO + i) * 8, 8), :] = tile
        for side in range(2):
            tiles = []
            for i in range(HALO // 2):
                first = HALO + HALO * side + 2 * i
                tiles.append(
                    jnp.where(
                        low_half,
                        ax_ref[pl.ds(first * 8, 8), :],
                        ax_ref[pl.ds((first + 1) * 8, 8), :],
                    )
                )
            as_ref[iteration, side] = jnp.concatenate(tiles, axis=0).astype(BF16)
        sides_start(*edges, iteration)
        if iteration:
            d_square, rr, observed, _ = sums_get(SUM)
            step = rr / (d_square + observed)
            for g in range(GROUPS):
                d = planes_first(d_ref, g)
                for i in range(min(8, PLANES - 8 * g)):
                    p = 8 * g + i
                    out_sol[p] = out_sol[p] + step * d[i]
        if iteration == 0:
            for dist in range(1, HALO + 1):
                halo_take(ENS, dist, em_ref)
        def back(r, _):
            row = ax_ref[pl.ds(pl.multiple_of(r * 8, 8), 8), :]
            for g in range(GROUPS):
                at = row_tile(r, g)
                x_ref[at, :] = (em_ref[at, :] * row).astype(BF16).astype(F32)
            return 0

        passing, _ = localization(z_ref)
        lax.fori_loop(HALO, HALO + ROWS, back, 0)
        for k in range(PASSES - 1):
            inside = list(range(HALO + 1 + k, HALO + ROWS - 1 - k))
            for first in range(0, len(inside), 4):
                passing(k, *inside[first : first + 4])
        sides_wait(*edges, iteration)
        for side in range(2):
            arrived = ar_ref[iteration, side].astype(F32)
            for i in range(HALO // 2):
                first = (HALO + ROWS) * side + 2 * i
                packed = arrived[i * 8 : (i + 1) * 8, :]
                turned = pltpu.roll(packed, 4, 0)
                ax_ref[pl.ds(first * 8, 8), :] = jnp.where(low_half, packed, turned)
                ax_ref[pl.ds((first + 1) * 8, 8), :] = jnp.where(low_half, turned, packed)

        lax.fori_loop(0, HALO, back, 0)
        lax.fori_loop(HALO + ROWS, EXT, back, 0)
        for k in range(PASSES):

            def outside(i, _):
                base = 1 + k + (10 - 2 * k) * i
                passing(k, *(base + j for j in range(4)))
                return 0

            lax.fori_loop(0, 2, outside, 0)

        if iteration + 1 == ITERS:
            for g in range(GROUPS):
                rows = []
                for i in range(ROWS):
                    at = row_tile(HALO + i, g)
                    image = d_ref[at, :] + sea_rows(i) * z_ref[at, :]
                    rows.append(r_ref[at, :] - step * image)
                turned = jnp.stack(rows, axis=0).transpose(1, 0, 2)
                for i in range(min(8, PLANES - 8 * g)):
                    out_res[8 * g + i] = turned[i][:, :LONS]
            continue

        def image(r, carry):
            sea_row = s_ref[pl.ds(pl.multiple_of(r * 8, 8), 8), :]
            sums = list(carry)
            for g in range(GROUPS):
                at = row_tile(r + HALO, g)
                d, res = d_ref[at, :], r_ref[at, :]
                img = d + sea_row * z_ref[at, :]
                im_ref[at, :] = img
                x_ref[at, :] = img * sea_row
                terms = (d * img, res * res, res * img, img * img)
                sums = [total + fold(term, valid) for total, term in zip(sums, terms)]
            return tuple(sums)

        sums_start(SUM, lax.fori_loop(0, ROWS, image, (jnp.zeros((8, 128), F32),) * 4))
        for dist in range(1, HALO + 1):
            halo_send(IMG, dist, masked(x_ref))
        halo_take(IMG, 1, x_ref)
        localize_stage(z_ref, 1)
        sums_pass_on(SUM)
        for stage in range(2, HALO + 1):
            halo_take(IMG, stage, x_ref)
            localize_stage(z_ref, stage)
        d_image, rr, r_image, image_image = sums_get(SUM)
        first_step = rr / d_image
        fresh = rr - 2.0 * first_step * r_image + first_step * first_step * image_image
        beta = fresh / rr

    for i in range(1 + 3 * ITERS):
        ref = mr_ref.at[i, pl.ds(0, NM - 1)]
        pltpu.make_async_copy(ref, ref, m_send.at[i]).wait()
        ref = tr_ref.at[i, pl.ds(0, NT - 1)]
        pltpu.make_async_copy(ref, ref, t_send.at[i]).wait()
    for kind in range(4):
        for dist in range(1, HALO + 1):
            for copy in halo_piece(kind, dist):
                copy.wait_send()
    for group, many in ((edges, ITERS), (faces, 1)):
        for i in range(many):
            for copy in sides(*group, i):
                copy.wait_send()


def shards(
    solution,
    residual,
    direction,
    ensemble,
    east_rate,
    north_rate,
    sea_mask,
    pass_counts,
    obs_owner,
    obs_cell,
    obs_level,
    obs_variable,
    obs_error,
):
    def planes(x):
        return x.reshape(PLANES, ROWS, LONS)

    def row(x):
        return x.reshape(1, SEGMENT)

    exchanges = 1 + 3 * ITERS
    vmem = pl.BlockSpec(memory_space=pltpu.VMEM)
    hbm = pl.BlockSpec(memory_space=pltpu.HBM)
    planes_f32 = pltpu.VMEM((PLANES, ROWS, LONS), F32)
    row_i32 = pltpu.VMEM((1, SEGMENT), jnp.int32)
    field = pltpu.VMEM((EXT * PAD, WIDE), F32)
    band = pltpu.VMEM((EXT * 8, WIDE), F32)
    shape = jax.ShapeDtypeStruct((PLANES, ROWS, LONS), F32)
    sol, res = pl.pallas_call(
        body,
        out_shape=(shape, shape),
        in_specs=[hbm] * 7 + [pl.BlockSpec(memory_space=pltpu.SMEM)] + [hbm] * 5,
        out_specs=(vmem, vmem),
        scratch_shapes=[
            planes_f32,
            planes_f32,
            planes_f32,
            pltpu.VMEM((PLANES, ROWS, LONS), BF16),
            pltpu.VMEM((ROWS, LONS), F32),
            pltpu.VMEM((ROWS, LONS), F32),
            pltpu.VMEM((ROWS, LONS), jnp.int32),
            row_i32,
            row_i32,
            row_i32,
            row_i32,
            pltpu.VMEM((1, SEGMENT), F32),
            pltpu.SemaphoreType.DMA((12,)),
            field,
            field,
            field,
            field,
            field,
            field,
            field,
            field,
            field,
            field,
            field,
            band,
            band,
            band,
            band,
            pltpu.VMEM((ROWS * 8, WIDE), F32),
            pltpu.VMEM((NM, 64, 256), BF16),
            pltpu.VMEM((NM, 256, SLOTS * 128), BF16),
            pltpu.VMEM((DEVS, 128), jnp.int32),
            pltpu.VMEM((DEVS, 128), F32),
            pltpu.VMEM((DEVS, 128), F32),
            pltpu.VMEM((NM, 64, 256), F32),
            pltpu.VMEM((64, WIDE), F32),
            band,
            pltpu.VMEM((DEVS, SEGMENT), BF16),
            pltpu.VMEM((2 * NT, SEGMENT), F32),
            pltpu.VMEM((PASSES, 8, 128), F32),
            pltpu.VMEM((4, 2, HALO, PAD, WIDE), BF16),
            pltpu.VMEM((4, 2, HALO, PAD, WIDE), BF16),
            pltpu.VMEM((ITERS, 2, 16, WIDE), BF16),
            pltpu.VMEM((ITERS, 2, 16, WIDE), BF16),
            pltpu.VMEM((1, 2, 8, WIDE), F32),
            pltpu.VMEM((1, 2, 8, WIDE), F32),
            pltpu.VMEM((exchanges, NM, NT, 128), F32),
            pltpu.VMEM((exchanges, NM, NT, 128), F32),
            pltpu.VMEM((exchanges, NT, 1, 128), F32),
            pltpu.VMEM((exchanges, NT, 1, 128), F32),
            pltpu.SemaphoreType.DMA((4, HALO, 2)),
            pltpu.SemaphoreType.DMA((4, HALO, 2)),
            pltpu.SemaphoreType.DMA((ITERS, 2)),
            pltpu.SemaphoreType.DMA((ITERS, 2)),
            pltpu.SemaphoreType.DMA((1, 2)),
            pltpu.SemaphoreType.DMA((1, 2)),
            pltpu.SemaphoreType.DMA((exchanges,)),
            pltpu.SemaphoreType.DMA((exchanges,)),
            pltpu.SemaphoreType.DMA((exchanges,)),
            pltpu.SemaphoreType.DMA((exchanges,)),
        ],
        compiler_params=pltpu.CompilerParams(
            collective_id=0, has_side_effects=True, vmem_limit_bytes=LIMIT
        ),
    )(
        planes(direction),
        planes(residual),
        planes(solution),
        planes(ensemble),
        east_rate,
        north_rate,
        sea_mask,
        pass_counts,
        row(obs_owner),
        row(obs_cell),
        row(obs_level),
        row(obs_variable),
        row(obs_error),
    )
    return sol.reshape(solution.shape), res.reshape(solution.shape)


def solution(mesh):
    return jax.shard_map(
        shards,
        mesh=mesh,
        in_specs=(
            P("mem", None, "tile", None),
            P("mem", None, "tile", None),
            P("mem", None, "tile", None),
            P("mem", None, "tile", None),
            P("tile", None),
            P("tile", None),
            P("tile", None),
            P(),
            P(("mem", "tile"), None),
            P(("mem", "tile")),
            P(("mem", "tile")),
            P(("mem", "tile")),
            P(("mem", "tile")),
        ),
        out_specs=(P("mem", None, "tile", None), P("mem", None, "tile", None)),
        check_vma=False,
    )
```

```python
import functools
import math

import jax
import jax.numpy as jnp
from jax import lax
from jax.experimental import pallas as pl
from jax.experimental.pallas import tpu as pltpu
from jax.sharding import PartitionSpec as P

MESH = pl.DeviceIdType.MESH
F32 = jnp.float32
BF16 = jnp.bfloat16

FIELDS = 4
LEVELS = 2
PASSES = 4
ITERS = 2
CORRELATION = 0.6
MEMBERS_DEV = 5
MEMBERS = 40
ROWS = 8
LONS = 1440
BLOCK = 180
SLOTS = 16
SEGMENT = 1024
NM = 8
NT = 16

HALO = 4
EXT = ROWS + 2 * HALO
PLANES = MEMBERS_DEV * FIELDS
PAD = 24
GROUPS = PAD // 8
WIDE = 1536
OWN = HALO * PAD
EDGE = HALO * PAD
DEVS = NM * NT
LIMIT = 60 * 1024 * 1024
TILES = WIDE // 128

IDS = 0


def widen(x):
    return jnp.concatenate([x, x[:, :64], x[:, 1408:1440]], axis=1)


def split(x):
    high = x.astype(BF16).astype(F32)
    return high, x - high


def fold(x, valid):
    total = x[:, 0:128]
    for k in range(1, WIDE // 128 - 1):
        total = total + x[:, 128 * k : 128 * (k + 1)]
    return total + x[:, WIDE - 128 : WIDE] * valid


def cols_of(j):
    return slice(128 * j, 128 * (j + 1))


def row_tile(r, g=0):
    return pl.ds(pl.multiple_of(r * PAD + g * 8, 8), 8)


def body(
    dir_hbm,
    res_hbm,
    sol_hbm,
    ens_hbm,
    east_hbm,
    north_hbm,
    sea_hbm,
    counts_ref,
    owner_hbm,
    cell_hbm,
    level_hbm,
    variable_hbm,
    error_hbm,
    out_sol,
    out_res,
    dir_ref,
    res_ref,
    sol_ref,
    ens_ref,
    east_ref,
    north_ref,
    sea_ref,
    owner_ref,
    cell_ref,
    level_ref,
    variable_ref,
    error_ref,
    load_sem,
    d_ref,
    r_ref,
    im_ref,
    x_ref,
    p1_ref,
    p2_ref,
    p3_ref,
    z_ref,
    l0_ref,
    lr_ref,
    em_ref,
    e_ref,
    n_ref,
    w_ref,
    k_ref,
    s_ref,
    lb_ref,
    oh_ref,
    rf_ref,
    ct_ref,
    pk_ref,
    ob_ref,
    adj_ref,
    ax_ref,
    one_q,
    one_t,
    pass_ref,
    hs_ref,
    hr_ref,
    as_ref,
    ar_ref,
    cs_ref,
    cr_ref,
    ms_ref,
    mr_ref,
    ts_ref,
    tr_ref,
    h_send,
    h_recv,
    a_send,
    a_recv,
    c_send,
    c_recv,
    m_send,
    m_recv,
    t_send,
    t_recv,
):
    m = lax.axis_index("mem")
    t = lax.axis_index("tile")
    up = lax.rem(t + 1, NT)
    down = lax.rem(t + NT - 1, NT)
    weight = 1.0 / math.sqrt(MEMBERS - 1)

    loads = {}
    for i, (name, source, target) in enumerate(
        (
            ("dir", dir_hbm, dir_ref),
            ("sea", sea_hbm, sea_ref),
            ("east", east_hbm, east_ref),
            ("north", north_hbm, north_ref),
            ("owner", owner_hbm, owner_ref),
            ("cell", cell_hbm, cell_ref),
            ("level", level_hbm, level_ref),
            ("variable", variable_hbm, variable_ref),
            ("error", error_hbm, error_ref),
            ("ens", ens_hbm, ens_ref),
            ("res", res_hbm, res_ref),
            ("sol", sol_hbm, sol_ref),
        )
    ):
        loads[name] = pltpu.make_async_copy(source, target, load_sem.at[i])
        loads[name].start()

    def loaded(*which):
        for name in which:
            loads[name].wait()

    barrier = pltpu.get_barrier_semaphore()

    def greet_mem(k, _):
        pl.semaphore_signal(
            barrier, inc=1, device_id=(lax.rem(m + k, NM), t), device_id_type=MESH
        )
        return 0

    def greet_tile(k, _):
        pl.semaphore_signal(
            barrier, inc=1, device_id=(m, lax.rem(t + k, NT)), device_id_type=MESH
        )
        return 0

    lax.fori_loop(1, NM, greet_mem, 0)
    lax.fori_loop(1, NT, greet_tile, 0)

    def mem_start(i, pick):
        def one(k, _):
            peer = lax.rem(m + k, NM)
            pltpu.make_async_remote_copy(
                src_ref=ms_ref.at[i, peer if pick else 0],
                dst_ref=mr_ref.at[i, m],
                send_sem=m_send.at[i],
                recv_sem=m_recv.at[i],
                device_id=(peer, t),
                device_id_type=MESH,
            ).start()
            return 0

        lax.fori_loop(1, NM, one, 0)
        mr_ref[i, m] = ms_ref[i, m if pick else 0]

    def mem_wait(i):
        ref = mr_ref.at[i, pl.ds(0, NM - 1)]
        pltpu.make_async_copy(ref, ref, m_recv.at[i]).wait()

    def tile_start(i, pick):
        def one(k, _):
            peer = lax.rem(t + k, NT)
            pltpu.make_async_remote_copy(
                src_ref=ts_ref.at[i, peer if pick else 0],
                dst_ref=tr_ref.at[i, t],
                send_sem=t_send.at[i],
                recv_sem=t_recv.at[i],
                device_id=(m, peer),
                device_id_type=MESH,
            ).start()
            return 0

        lax.fori_loop(1, NT, one, 0)
        tr_ref[i, t] = ts_ref[i, t if pick else 0]

    def tile_wait(i):
        ref = tr_ref.at[i, pl.ds(0, NT - 1)]
        pltpu.make_async_copy(ref, ref, t_recv.at[i]).wait()

    def sides(send, recv, ssem, rsem, i):
        low = pltpu.make_async_remote_copy(
            src_ref=send.at[i, 0],
            dst_ref=recv.at[i, 1],
            send_sem=ssem.at[i, 0],
            recv_sem=rsem.at[i, 1],
            device_id=(m, down),
            device_id_type=MESH,
        )
        high = pltpu.make_async_remote_copy(
            src_ref=send.at[i, 1],
            dst_ref=recv.at[i, 0],
            send_sem=ssem.at[i, 1],
            recv_sem=rsem.at[i, 0],
            device_id=(m, up),
            device_id_type=MESH,
        )
        return low, high

    def sides_start(*which):
        for copy in sides(*which):
            copy.start()

    def sides_wait(*which):
        for copy in sides(*which):
            copy.wait_recv()

    edges = (as_ref, ar_ref, a_send, a_recv)
    faces = (cs_ref, cr_ref, c_send, c_recv)
    DIR, ENS, RES, IMG = 0, 1, 2, 3

    def halo_piece(kind, dist):
        low = pltpu.make_async_remote_copy(
            src_ref=hs_ref.at[kind, 0, dist - 1],
            dst_ref=hr_ref.at[kind, 1, dist - 1],
            send_sem=h_send.at[kind, dist - 1, 0],
            recv_sem=h_recv.at[kind, dist - 1, 1],
            device_id=(m, down),
            device_id_type=MESH,
        )
        high = pltpu.make_async_remote_copy(
            src_ref=hs_ref.at[kind, 1, dist - 1],
            dst_ref=hr_ref.at[kind, 0, dist - 1],
            send_sem=h_send.at[kind, dist - 1, 1],
            recv_sem=h_recv.at[kind, dist - 1, 0],
            device_id=(m, up),
            device_id_type=MESH,
        )
        return low, high

    def below_row(dist):
        return HALO - dist

    def above_row(dist):
        return HALO + ROWS - 1 + dist

    def whole_row(r):
        return pl.ds(r * PAD, PAD)

    def halo_send(kind, dist, row_of):
        hs_ref[kind, 0, dist - 1] = row_of(HALO + dist - 1).astype(BF16)
        hs_ref[kind, 1, dist - 1] = row_of(HALO + ROWS - dist).astype(BF16)
        for copy in halo_piece(kind, dist):
            copy.start()

    def halo_take(kind, dist, dst):
        for copy in halo_piece(kind, dist):
            copy.wait_recv()
        dst[whole_row(below_row(dist)), :] = hr_ref[kind, 0, dist - 1].astype(F32)
        dst[whole_row(above_row(dist)), :] = hr_ref[kind, 1, dist - 1].astype(F32)

    sub = lax.broadcasted_iota(jnp.int32, (8, WIDE), 0)
    lane = lax.broadcasted_iota(jnp.int32, (8, 128), 1)
    valid = (lane < LONS - (WIDE - 128)).astype(F32)
    sub_small = lax.broadcasted_iota(jnp.int32, (8, 128), 0)
    low_half = sub < 4
    is_first, is_last = lane == 0, lane == 127

    loaded("sea", "east", "north")
    sea = widen(sea_ref[...].astype(F32))
    east = widen(east_ref[...])
    north = widen(north_ref[...])
    sea_up = pltpu.roll(sea, 7, 0)
    east_face = east * sea * pltpu.roll(sea, WIDE - 1, 1)
    north_raw = north * sea
    north_face = jnp.where(sub < 7, north_raw * sea_up, north_raw)
    cs_ref[0, 1] = jnp.where(low_half, pltpu.roll(east_face, 4, 0), north_face)
    cs_ref[0, 0] = jnp.where(
        low_half, east_face, jnp.where(sub < 7, pltpu.roll(north_face, 4, 0), sea_up)
    )

    def spread_row(value, i):
        return jnp.broadcast_to(value[i : i + 1, :], (8, WIDE))

    for i in range(ROWS):
        e_ref[pl.ds((HALO + i) * 8, 8), :] = spread_row(east_face, i)
        n_ref[pl.ds((HALO + i) * 8, 8), :] = spread_row(north_face, i)
        s_ref[pl.ds(i * 8, 8), :] = spread_row(sea, i)

    field_of = lax.rem(sub_small, 4)
    c0, c1, c2, c3 = (counts_ref[0], counts_ref[1], counts_ref[2], counts_ref[3])
    count = jnp.where(
        field_of == 0, c0, jnp.where(field_of == 1, c1, jnp.where(field_of == 2, c2, c3))
    )
    for k in range(PASSES):
        pass_ref[k] = (count > k).astype(F32)

    zero_tile = jnp.zeros((8, WIDE), F32)

    def rows_first(ref, g):
        parts = [widen(ref[8 * g + i].astype(F32)) for i in range(min(8, PLANES - 8 * g))]
        parts += [zero_tile] * (8 - len(parts))
        return jnp.stack(parts, axis=0).transpose(1, 0, 2)

    def planes_first(ref, g):
        rows = jnp.stack([ref[row_tile(HALO + i, g), :] for i in range(ROWS)], axis=0)
        return rows.transpose(1, 0, 2)[:, :, :LONS]

    def sea_rows(r):
        return s_ref[pl.ds(pl.multiple_of(r * 8, 8), 8), :]

    loaded("dir")
    for g in range(GROUPS):
        turned = rows_first(dir_ref, g)
        for i in range(ROWS):
            d_ref[row_tile(HALO + i, g), :] = turned[i]
            x_ref[row_tile(HALO + i, g), :] = turned[i] * sea_rows(i)

    pl.semaphore_wait(barrier, NM + NT - 2)

    sides_start(*faces, 0)

    def masked(ref):
        return lambda r: ref[whole_row(r), :]

    halo_send(DIR, 1, masked(x_ref))

    loaded("owner", "cell", "level", "variable", "error")
    owner = owner_ref[...]
    cell = cell_ref[...].astype(F32)
    cell_row = jnp.floor((cell + 0.5) * (1.0 / BLOCK))
    col_id = cell - cell_row * BLOCK
    rf_id = cell_row * FIELDS + (variable_ref[...] * LEVELS + level_ref[...]).astype(F32)
    inv_err = 1.0 / error_ref[...]
    owner_tile = lax.rem(owner, NT)
    owner_mem = owner // NT
    dev_iota = lax.broadcasted_iota(jnp.int32, (DEVS, SEGMENT), 0)
    owns = jnp.where(dev_iota == owner, 1.0, 0.0)
    before = jnp.where(
        lax.broadcasted_iota(jnp.int32, (SEGMENT, SEGMENT), 0)
        < lax.broadcasted_iota(jnp.int32, (SEGMENT, SEGMENT), 1),
        1.0,
        0.0,
    ).astype(BF16)
    ranks = jnp.dot(owns.astype(BF16), before, preferred_element_type=F32)
    slot = jnp.sum(ranks * owns, axis=0, keepdims=True).astype(jnp.int32)
    place = owner_mem * SLOTS + slot
    one_q[...] = jnp.where(dev_iota == place, 1.0, 0.0).astype(BF16)
    t_iota = lax.rem(lax.broadcasted_iota(jnp.int32, (2 * NT, SEGMENT), 0), NT)
    t_is_high = lax.broadcasted_iota(jnp.int32, (2 * NT, SEGMENT), 0) < NT
    one_t[...] = jnp.where(t_iota == owner_tile, 1.0, 0.0)

    def to_table(high, low):
        left = one_t[...] * jnp.where(t_is_high, high, low)
        return lax.dot_general(
            left.astype(BF16), one_q[...], (((1,), (1,)), ((), ())), preferred_element_type=F32
        )

    def tile_rows(i, table):
        for k in range(NT):
            ts_ref[i, k] = table[k : k + 1, :]

    def tile_table(i):
        return jnp.concatenate([tr_ref[i, k] for k in range(NT)], axis=0)

    table = to_table(col_id, rf_id)
    tile_rows(IDS, table[NT:] * 256.0 + table[:NT])

    tile_start(IDS, True)
    halo_send(DIR, 2, masked(x_ref))
    halo_send(DIR, 3, masked(x_ref))
    halo_send(DIR, 4, masked(x_ref))

    loaded("res")
    for g in range(GROUPS):
        turned = rows_first(res_ref, g)
        for i in range(ROWS):
            r_ref[row_tile(HALO + i, g), :] = turned[i]
            lr_ref[row_tile(HALO + i, g), :] = turned[i] * sea_rows(i)
    for dist in range(1, HALO + 1):
        halo_send(RES, dist, masked(lr_ref))

    loaded("ens")
    for g in range(GROUPS):
        turned = rows_first(ens_ref, g)
        for i in range(ROWS):
            em_ref[row_tile(HALO + i, g), :] = turned[i] * sea_rows(i)

    sides_wait(*faces, 0)
    below, above = cr_ref[0, 0], cr_ref[0, 1]
    not_first = jnp.where(t > 0, 1.0, 0.0)
    not_last = jnp.where(t < NT - 1, 1.0, 0.0)
    for i in range(HALO):
        e_ref[pl.ds(i * 8, 8), :] = spread_row(below, i)
        e_ref[pl.ds((HALO + ROWS + i) * 8, 8), :] = spread_row(above, i)
    for i in range(HALO - 1):
        n_ref[pl.ds(i * 8, 8), :] = spread_row(below, HALO + i)
        n_ref[pl.ds((HALO + ROWS + i) * 8, 8), :] = spread_row(above, HALO + i)
    n_ref[pl.ds((HALO - 1) * 8, 8), :] = (
        spread_row(below, 2 * HALO - 1) * s_ref[pl.ds(0, 8), :] * not_first
    )
    n_ref[pl.ds((HALO + ROWS - 1) * 8, 8), :] = (
        n_ref[pl.ds((HALO + ROWS - 1) * 8, 8), :] * spread_row(above, 2 * HALO - 1) * not_last
    )

    for r in range(1, EXT - 1):
        here = pl.ds(r * 8, 8)
        e, n, s = e_ref[here, :], n_ref[here, :], n_ref[pl.ds((r - 1) * 8, 8), :]
        w = pltpu.roll(e, 1, 1)
        w_ref[here, :] = w
        k_ref[here, :] = 1.0 - e - w - n - s

    levels = (x_ref, p1_ref, p2_ref, p3_ref)

    def localization(result):
        def passing(k, *rows):
            src = levels[k]
            dst = levels[k + 1] if k + 1 < PASSES else result
            keep = jnp.broadcast_to(pass_ref[k][:, 0:1], (8, 128)) > 0.0

            def row(r):
                here8 = pl.multiple_of(r * 8, 8)
                back8 = pl.multiple_of((r - 1) * 8, 8)
                ats = [(row_tile(r, g), row_tile(r + 1, g), row_tile(r - 1, g)) for g in range(GROUPS)]
                near, far, last = [], [], []
                for at, _, _ in ats:
                    v = src[at, cols_of(0)]
                    near.append((v, pltpu.roll(v, 1, 1), pltpu.roll(v, 127, 1)))
                    last.append(pltpu.roll(src[at, cols_of(TILES - 1)], 1, 1))
                first_east = [x[2] for x in near]
                for j in range(TILES):
                    cols = cols_of(j)
                    here, back = pl.ds(here8, 8), pl.ds(back8, 8)
                    ck, ce, cw = k_ref[here, cols], e_ref[here, cols], w_ref[here, cols]
                    cn, cs = n_ref[here, cols], n_ref[back, cols]
                    for g, (at, over, under) in enumerate(ats):
                        v, west, east = near[g]
                        if j < TILES - 1:
                            ahead = src[at, cols_of(j + 1)]
                            following = (ahead, pltpu.roll(ahead, 1, 1), pltpu.roll(ahead, 127, 1))
                            next_east = following[2]
                        else:
                            following, next_east = None, first_east[g]
                        total = (
                            ck * v
                            + ce * jnp.where(is_last, next_east, east)
                            + cw * jnp.where(is_first, last[g], west)
                            + cn * src[over, cols]
                            + cs * src[under, cols]
                        )
                        dst[at, cols] = jnp.where(keep, total, v)
                        near[g], last[g] = following, west

            for r in rows:
                row(r)

        def across(k, low, high):
            def quad(i, _):
                passing(k, *(low + 4 * i + j for j in range(4)))
                return 0

            whole = (high - low) // 4
            lax.fori_loop(0, whole, quad, 0)
            if low + 4 * whole < high:
                passing(k, *range(low + 4 * whole, high))

        return passing, across

    def localize_pass(result, k):
        localization(result)[1](k, 1 + k, EXT - 1 - k)

    def localize(result):
        for k in range(PASSES):
            localize_pass(result, k)

    def localize_stage(result, stage):
        passing, across = localization(result)
        for k in range(stage):
            dist = stage - 1 - k
            if dist:
                passing(k, below_row(dist), above_row(dist))
            else:
                across(k, HALO, HALO + ROWS)


    col_iota = lax.broadcasted_iota(jnp.int32, (256, 128), 0).astype(F32).astype(BF16)
    ones, zeros = jnp.ones((256, 128), BF16), jnp.zeros((256, 128), BF16)

    def build_one_hots():
        mem_wait(IDS)
        ids = mr_ref[IDS].reshape(DEVS, DEVS).T
        rf_all = jnp.floor(ids * (1.0 / 256.0))
        rf_ref[...] = rf_all.astype(jnp.int32)
        ct_ref[...] = ids - rf_all * 256.0

        def build(b, _):
            cols = ct_ref[pl.ds(pl.multiple_of(b * SLOTS, SLOTS), SLOTS), :]
            for s in range(SLOTS):
                same = jnp.broadcast_to(cols[s : s + 1, :], (16, 128)).astype(BF16)
                same = jnp.concatenate([same] * 16, axis=0)
                oh_ref[b, :, s * 128 : (s + 1) * 128] = jnp.where(col_iota == same, ones, zeros)
            return 0

        lax.fori_loop(0, NM, build, 0)

    row_key = lax.broadcasted_iota(jnp.int32, (64, 128), 0)
    key = (row_key // 8) * FIELDS + lax.rem(row_key, 4)
    is_high = lax.rem(row_key, 8) < 4

    def window(b):
        start = BLOCK * b
        first = (start // 128) * 128
        return first, start - first

    segment = lax.broadcasted_iota(jnp.int32, (1, 128), 1) // 32

    def sums_start(i, totals):
        packed = jnp.zeros((1, 128), F32)
        for k, total in enumerate(totals):
            total = jnp.sum(total, axis=0, keepdims=True)
            total = total + pltpu.roll(total, 64, 1)
            total = total + pltpu.roll(total, 32, 1)
            packed = jnp.where(segment == k, total, packed)
        ts_ref[i, 0] = packed
        tile_start(i, False)

    def sums_pass_on(i):
        tile_wait(i)
        part = tr_ref[i, 0]
        for k in range(1, NT):
            part = part + tr_ref[i, k]
        ms_ref[i, 0] = jnp.broadcast_to(part, (NT, 128))
        mem_start(i, False)

    def sums_get(i):
        mem_wait(i)
        total = mr_ref[i, 0, pl.ds(0, 8), :]
        for k in range(1, NM):
            total = total + mr_ref[i, k, pl.ds(0, 8), :]
        total = total[0:1, :]
        return [
            jnp.sum(jnp.where(segment == k, total, 0.0), axis=1, keepdims=True) for k in range(4)
        ]

    for iteration in range(ITERS):
        base = 1 + 3 * iteration
        PICK, WGT, SUM = base, base + 1, base + 2
        if iteration == 0:
            for stage in range(1, HALO + 1):
                halo_take(DIR, stage, x_ref)
                localize_stage(l0_ref, stage)
                if stage == 2:
                    tile_wait(IDS)
                    ms_ref[IDS, 0] = tile_table(IDS)
                    mem_start(IDS, False)
            build_one_hots()

        def partial(r, _):
            total = zero_tile
            for g in range(GROUPS):
                at = row_tile(r + HALO, g)
                field = l0_ref[at, :]
                if iteration:
                    field = lr_ref[at, :] - first_step * z_ref[at, :] + beta * field
                total = total + em_ref[at, :] * field.astype(BF16).astype(F32)
            total = total + pltpu.roll(total, 4, 0)
            high, low = split(total)
            adj_ref[pl.ds(pl.multiple_of(r * 8, 8), 8), :] = jnp.where(low_half, high, low)
            return 0

        lax.fori_loop(0, ROWS, partial, 0)
        for b in range(NM):
            first, shift = window(b)
            piece = adj_ref[:, first : first + 384]
            if shift:
                piece = pltpu.roll(piece, 384 - shift, 1)
            lb_ref[b] = piece[:, :256].astype(BF16)

        def gather(b, _):
            got = jnp.dot(lb_ref[b], oh_ref[b], preferred_element_type=F32)
            rows16 = pl.ds(pl.multiple_of(b * SLOTS, SLOTS), SLOTS)
            wanted = rf_ref[rows16, :]
            rows = []
            for s in range(SLOTS):
                part = jnp.where(
                    key == wanted[s : s + 1, :], got[:, s * 128 : (s + 1) * 128], 0.0
                )
                rows.append(jnp.sum(part, axis=0, keepdims=True))
            pk_ref[rows16, :] = jnp.concatenate(rows, axis=0)
            return 0

        lax.fori_loop(0, NM, gather, 0, unroll=2)
        ms_ref[PICK] = pk_ref[...].T.reshape(NM, NT, 128)
        mem_start(PICK, True)
        if iteration == 0:
            x_ref[pl.ds(OWN, ROWS * PAD), :] = lr_ref[pl.ds(OWN, ROWS * PAD), :]
            for dist in range(1, HALO + 1):
                halo_take(RES, dist, x_ref)
            localize_pass(lr_ref, 0)
        else:

            def turn(r, carry):
                rr, dd = carry
                for g in range(GROUPS):
                    at = row_tile(r + HALO, g)
                    res = r_ref[at, :] - first_step * im_ref[at, :]
                    d = res + beta * d_ref[at, :]
                    r_ref[at, :] = res
                    d_ref[at, :] = d
                    rr, dd = rr + fold(res * res, valid), dd + fold(d * d, valid)
                return rr, dd

            own_rr, own_dd = lax.fori_loop(0, ROWS, turn, (jnp.zeros((8, 128), F32),) * 2)
        mem_wait(PICK)
        summed = mr_ref[PICK, 0]
        for k in range(1, NM):
            summed = summed + mr_ref[PICK, k]
        tile_rows(PICK, summed * weight)
        tile_start(PICK, True)
        if iteration == 0:
            halo_send(ENS, 1, masked(em_ref))
            halo_send(ENS, 2, masked(em_ref))
            localize_pass(lr_ref, 1)
        else:
            loaded("sol")
            for p in range(PLANES):
                out_sol[p] = sol_ref[p] + first_step * dir_ref[p]
        tile_wait(PICK)

        high, low = split(tile_table(PICK))
        both = jnp.concatenate([high, low], axis=0).astype(BF16)
        seen = jnp.dot(both, one_q[...], preferred_element_type=F32)
        value = jnp.sum(seen * one_t[...], axis=0, keepdims=True)
        u = value * inv_err
        along = lax.broadcasted_iota(jnp.int32, (1, SEGMENT), 1)
        following = jnp.where(along == SEGMENT - 1, 0.0, pltpu.roll(u, SEGMENT - 1, 1))
        preceding = jnp.where(along == 0, 0.0, pltpu.roll(u, 1, 1))
        ends = ((along == 0) | (along == SEGMENT - 1)).astype(F32)
        square = CORRELATION * CORRELATION
        mixed = ((1.0 + square - square * ends) * u - CORRELATION * (following + preceding)) / (
            1.0 - square
        )
        weighted = mixed * inv_err
        high, low = split(weighted)
        table = to_table(high, low)
        tile_rows(WGT, table[:NT] + table[NT:])
        tile_start(WGT, True)
        if iteration == 0:
            halo_send(ENS, 3, masked(em_ref))
            halo_send(ENS, 4, masked(em_ref))
        else:
            product = value * weighted
            observed = product[:, 0:128]
            for k in range(1, SEGMENT // 128):
                observed = observed + product[:, 128 * k : 128 * (k + 1)]
            sums_start(SUM, (own_dd, own_rr, observed))
        if iteration == 0:
            localize_pass(lr_ref, 2)
        tile_wait(WGT)
        ms_ref[WGT, 0] = tile_table(WGT)
        mem_start(WGT, False)
        if iteration == 0:
            localize_pass(lr_ref, 3)
        else:
            sums_pass_on(SUM)
        mem_wait(WGT)
        pk_ref[...] = mr_ref[WGT].reshape(DEVS, DEVS).T

        def scatter(b, _):
            rows16 = pl.ds(pl.multiple_of(b * SLOTS, SLOTS), SLOTS)
            wanted = rf_ref[rows16, :]
            high, low = split(pk_ref[rows16, :])
            parts = []
            for s in range(SLOTS):
                row = jnp.where(is_high, high[s : s + 1, :], low[s : s + 1, :])
                parts.append(jnp.where(key == wanted[s : s + 1, :], row, 0.0).astype(BF16))
            ob_ref[b] = lax.dot_general(
                jnp.concatenate(parts, axis=1),
                oh_ref[b],
                (((1,), (1,)), ((), ())),
                preferred_element_type=F32,
            )
            return 0

        lax.fori_loop(0, NM, scatter, 0, unroll=2)
        adj_ref[...] = jnp.zeros((64, WIDE), F32)
        for b in range(NM):
            first, shift = window(b)
            piece = jnp.concatenate([ob_ref[b], jnp.zeros((64, 128), F32)], axis=1)
            if shift:
                piece = pltpu.roll(piece, shift, 1)
            adj_ref[:, first : first + 384] = adj_ref[:, first : first + 384] + piece
        lane64 = lax.broadcasted_iota(jnp.int32, (64, 128), 1)
        head, tail = adj_ref[:, 0:128], adj_ref[:, WIDE - 128 : WIDE]
        adj_ref[:, WIDE - 128 : WIDE] = jnp.where(
            lane64 < 32, tail, jnp.where(lane64 < 96, pltpu.roll(head, 32, 1), pltpu.roll(tail, 96, 1))
        )
        own_rows = []
        for i in range(ROWS):
            tile = adj_ref[pl.ds(i * 8, 8), :]
            tile = (tile + pltpu.roll(tile, 4, 0)) * weight
            ax_ref[pl.ds((HALO + i) * 8, 8), :] = tile
        for side in range(2):
            tiles = []
            for i in range(HALO // 2):
                first = HALO + HALO * side + 2 * i
                tiles.append(
                    jnp.where(
                        low_half,
                        ax_ref[pl.ds(first * 8, 8), :],
                        ax_ref[pl.ds((first + 1) * 8, 8), :],
                    )
                )
            as_ref[iteration, side] = jnp.concatenate(tiles, axis=0).astype(BF16)
        sides_start(*edges, iteration)
        if iteration:
            d_square, rr, observed, _ = sums_get(SUM)
            step = rr / (d_square + observed)
            for g in range(GROUPS):
                d = planes_first(d_ref, g)
                for i in range(min(8, PLANES - 8 * g)):
                    p = 8 * g + i
                    out_sol[p] = out_sol[p] + step * d[i]
        if iteration == 0:
            for dist in range(1, HALO + 1):
                halo_take(ENS, dist, em_ref)
        def back(r, _):
            row = ax_ref[pl.ds(pl.multiple_of(r * 8, 8), 8), :]
            for g in range(GROUPS):
                at = row_tile(r, g)
                x_ref[at, :] = (em_ref[at, :] * row).astype(BF16).astype(F32)
            return 0

        passing, _ = localization(z_ref)
        lax.fori_loop(HALO, HALO + ROWS, back, 0)
        for k in range(PASSES - 1):
            inside = list(range(HALO + 1 + k, HALO + ROWS - 1 - k))
            for first in range(0, len(inside), 4):
                passing(k, *inside[first : first + 4])
        sides_wait(*edges, iteration)
        for side in range(2):
            arrived = ar_ref[iteration, side].astype(F32)
            for i in range(HALO // 2):
                first = (HALO + ROWS) * side + 2 * i
                packed = arrived[i * 8 : (i + 1) * 8, :]
                turned = pltpu.roll(packed, 4, 0)
                ax_ref[pl.ds(first * 8, 8), :] = jnp.where(low_half, packed, turned)
                ax_ref[pl.ds((first + 1) * 8, 8), :] = jnp.where(low_half, turned, packed)

        lax.fori_loop(0, HALO, back, 0)
        lax.fori_loop(HALO + ROWS, EXT, back, 0)
        for k in range(PASSES):

            def outside(i, _):
                base = 1 + k + (10 - 2 * k) * i
                passing(k, *(base + j for j in range(4)))
                return 0

            lax.fori_loop(0, 2, outside, 0)

        if iteration + 1 == ITERS:
            for g in range(GROUPS):
                rows = []
                for i in range(ROWS):
                    at = row_tile(HALO + i, g)
                    image = d_ref[at, :] + sea_rows(i) * z_ref[at, :]
                    rows.append(r_ref[at, :] - step * image)
                turned = jnp.stack(rows, axis=0).transpose(1, 0, 2)
                for i in range(min(8, PLANES - 8 * g)):
                    out_res[8 * g + i] = turned[i][:, :LONS]
            continue

        def image(r, carry):
            sea_row = s_ref[pl.ds(pl.multiple_of(r * 8, 8), 8), :]
            sums = list(carry)
            for g in range(GROUPS):
                at = row_tile(r + HALO, g)
                d, res = d_ref[at, :], r_ref[at, :]
                img = d + sea_row * z_ref[at, :]
                im_ref[at, :] = img
                x_ref[at, :] = img * sea_row
                terms = (d * img, res * res, res * img, img * img)
                sums = [total + fold(term, valid) for total, term in zip(sums, terms)]
            return tuple(sums)

        sums_start(SUM, lax.fori_loop(0, ROWS, image, (jnp.zeros((8, 128), F32),) * 4))
        for dist in range(1, HALO + 1):
            halo_send(IMG, dist, masked(x_ref))
        halo_take(IMG, 1, x_ref)
        localize_stage(z_ref, 1)
        sums_pass_on(SUM)
        for stage in range(2, HALO + 1):
            halo_take(IMG, stage, x_ref)
            localize_stage(z_ref, stage)
        d_image, rr, r_image, image_image = sums_get(SUM)
        first_step = rr / d_image
        fresh = rr - 2.0 * first_step * r_image + first_step * first_step * image_image
        beta = fresh / rr

    for i in range(1 + 3 * ITERS):
        ref = mr_ref.at[i, pl.ds(0, NM - 1)]
        pltpu.make_async_copy(ref, ref, m_send.at[i]).wait()
        ref = tr_ref.at[i, pl.ds(0, NT - 1)]
        pltpu.make_async_copy(ref, ref, t_send.at[i]).wait()
    for kind in range(4):
        for dist in range(1, HALO + 1):
            for copy in halo_piece(kind, dist):
                copy.wait_send()
    for group, many in ((edges, ITERS), (faces, 1)):
        for i in range(many):
            for copy in sides(*group, i):
                copy.wait_send()


def shards(
    solution,
    residual,
    direction,
    ensemble,
    east_rate,
    north_rate,
    sea_mask,
    pass_counts,
    obs_owner,
    obs_cell,
    obs_level,
    obs_variable,
    obs_error,
):
    def planes(x):
        return x.reshape(PLANES, ROWS, LONS)

    def row(x):
        return x.reshape(1, SEGMENT)

    exchanges = 1 + 3 * ITERS
    vmem = pl.BlockSpec(memory_space=pltpu.VMEM)
    hbm = pl.BlockSpec(memory_space=pltpu.HBM)
    planes_f32 = pltpu.VMEM((PLANES, ROWS, LONS), F32)
    row_i32 = pltpu.VMEM((1, SEGMENT), jnp.int32)
    field = pltpu.VMEM((EXT * PAD, WIDE), F32)
    band = pltpu.VMEM((EXT * 8, WIDE), F32)
    shape = jax.ShapeDtypeStruct((PLANES, ROWS, LONS), F32)
    sol, res = pl.pallas_call(
        body,
        out_shape=(shape, shape),
        in_specs=[hbm] * 7 + [pl.BlockSpec(memory_space=pltpu.SMEM)] + [hbm] * 5,
        out_specs=(vmem, vmem),
        scratch_shapes=[
            planes_f32,
            planes_f32,
            planes_f32,
            pltpu.VMEM((PLANES, ROWS, LONS), BF16),
            pltpu.VMEM((ROWS, LONS), F32),
            pltpu.VMEM((ROWS, LONS), F32),
            pltpu.VMEM((ROWS, LONS), jnp.int32),
            row_i32,
            row_i32,
            row_i32,
            row_i32,
            pltpu.VMEM((1, SEGMENT), F32),
            pltpu.SemaphoreType.DMA((12,)),
            field,
            field,
            field,
            field,
            field,
            field,
            field,
            field,
            field,
            field,
            field,
            band,
            band,
            band,
            band,
            pltpu.VMEM((ROWS * 8, WIDE), F32),
            pltpu.VMEM((NM, 64, 256), BF16),
            pltpu.VMEM((NM, 256, SLOTS * 128), BF16),
            pltpu.VMEM((DEVS, 128), jnp.int32),
            pltpu.VMEM((DEVS, 128), F32),
            pltpu.VMEM((DEVS, 128), F32),
            pltpu.VMEM((NM, 64, 256), F32),
            pltpu.VMEM((64, WIDE), F32),
            band,
            pltpu.VMEM((DEVS, SEGMENT), BF16),
            pltpu.VMEM((2 * NT, SEGMENT), F32),
            pltpu.VMEM((PASSES, 8, 128), F32),
            pltpu.VMEM((4, 2, HALO, PAD, WIDE), BF16),
            pltpu.VMEM((4, 2, HALO, PAD, WIDE), BF16),
            pltpu.VMEM((ITERS, 2, 16, WIDE), BF16),
            pltpu.VMEM((ITERS, 2, 16, WIDE), BF16),
            pltpu.VMEM((1, 2, 8, WIDE), F32),
            pltpu.VMEM((1, 2, 8, WIDE), F32),
            pltpu.VMEM((exchanges, NM, NT, 128), F32),
            pltpu.VMEM((exchanges, NM, NT, 128), F32),
            pltpu.VMEM((exchanges, NT, 1, 128), F32),
            pltpu.VMEM((exchanges, NT, 1, 128), F32),
            pltpu.SemaphoreType.DMA((4, HALO, 2)),
            pltpu.SemaphoreType.DMA((4, HALO, 2)),
            pltpu.SemaphoreType.DMA((ITERS, 2)),
            pltpu.SemaphoreType.DMA((ITERS, 2)),
            pltpu.SemaphoreType.DMA((1, 2)),
            pltpu.SemaphoreType.DMA((1, 2)),
            pltpu.SemaphoreType.DMA((exchanges,)),
            pltpu.SemaphoreType.DMA((exchanges,)),
            pltpu.SemaphoreType.DMA((exchanges,)),
            pltpu.SemaphoreType.DMA((exchanges,)),
        ],
        compiler_params=pltpu.CompilerParams(
            collective_id=0, has_side_effects=True, vmem_limit_bytes=LIMIT
        ),
    )(
        planes(direction),
        planes(residual),
        planes(solution),
        planes(ensemble),
        east_rate,
        north_rate,
        sea_mask,
        pass_counts,
        row(obs_owner),
        row(obs_cell),
        row(obs_level),
        row(obs_variable),
        row(obs_error),
    )
    return sol.reshape(solution.shape), res.reshape(solution.shape)


def solution(mesh):
    return jax.shard_map(
        shards,
        mesh=mesh,
        in_specs=(
            P("mem", None, "tile", None),
            P("mem", None, "tile", None),
            P("mem", None, "tile", None),
            P("mem", None, "tile", None),
            P("tile", None),
            P("tile", None),
            P("tile", None),
            P(),
            P(("mem", "tile"), None),
            P(("mem", "tile")),
            P(("mem", "tile")),
            P(("mem", "tile")),
            P(("mem", "tile")),
        ),
        out_specs=(P("mem", None, "tile", None), P("mem", None, "tile", None)),
        check_vma=False,
    )
```
